32 devices in a mesh: dp: 4 (over x, core), sx: 2 (over y), sy: 4 (over z).
Axes of the slice: x: 2, y: 2, z: 4, core: 2. Of those that a mesh axis runs over, the one named last changes fastest.
Arguments:
- activations: bfloat16 [4, 16, 16, 2048], P('dp', 'sx', 'sy'), may hold values from -6 to 6
- preact: bfloat16 [4, 16, 16, 4096], P('dp', 'sx', 'sy'), may hold values from -6 to 6
- pooled_grad: bfloat16 [4, 8, 8, 2048], P('dp', 'sx', 'sy'), may hold values from -12 to 12
- weights: bfloat16 [27, 64, 128], replicated, may hold values from -0.109375 to 0.109375
Outputs:
- input_grad: bfloat16 [4, 16, 16, 2048], P('dp', 'sx', 'sy')
- weight_grad: float32 [27, 64, 128], replicated
- bias_grad: float32 [128], replicated
The draws below stay inside these ranges and needn't reach their ends.
All inputs are finite; a program needn't handle non-finite values.
Results may differ from the reference program's by a relative error of at most 0.0021.
Values may be sent and summed in bfloat16 or wider, within the bound.
A program may use at most 64 MiB of HBM per device.

```python
import jax
import jax.numpy as jnp
from jax import lax

CI = 64
CO = 128
SAMPLES = 4
NX = 16
NY = 16
NZ = 32


def steps_of(rng, extent, split, smallest, largest):
    def one(dim, blocks):
        draws = jax.random.uniform(jax.random.fold_in(jax.random.fold_in(rng, 6), dim), (blocks,), jnp.float32, smallest / len(split), largest / len(split))
        return jnp.repeat(jnp.exp(draws), extent[dim] // blocks).reshape((-1,) + (1,) * (len(extent) - dim - 1))

    gain = one(*split[0])
    for cut in split[1:]:
        gain = gain * one(*cut)
    return gain


def gaussian(key, extent, scale, reach, cuts=(), kind=jnp.bfloat16):
    gain = steps_of(key, extent, cuts, -0.22, 0.18) if cuts else 1.0
    drawn = jax.random.normal(key, extent, jnp.float32) * scale * gain
    return jnp.minimum(jnp.maximum(drawn, -reach), reach).astype(kind)


def setup_inputs(seed: int = 0) -> dict:
    seeds = jax.random.split(jax.random.key(seed), 5)
    activations = gaussian(seeds[0], (SAMPLES, NX, NY, NZ * CI), 1.0, 6.0, ((0, 4), (1, 2), (2, 4)))
    preact = gaussian(seeds[1], (SAMPLES, NX, NY, NZ * CO), 1.0, 6.0, ((0, 4), (1, 2), (2, 4)))
    pooled_grad = gaussian(seeds[2], (SAMPLES, NX // 2, NY // 2, (NZ // 2) * CO), 2.0, 12.0, ((0, 4), (1, 2), (2, 4)))
    weights = gaussian(seeds[3], (27, CI, CO), (27 * CO) ** -0.5, 0.109375)
    return dict(activations=activations, preact=preact, pooled_grad=pooled_grad, weights=weights)


stencil_offsets = [(ox, oy, oz) for ox in (-1, 0, 1) for oy in (-1, 0, 1) for oz in (-1, 0, 1)]


def reference(activations, preact, pooled_grad, weights):
    def per_sample(carry, items):
        weight_acc, bias_acc = carry
        acts, before, upper = items
        acts = acts.reshape(NX, NY, NZ, CI)
        upper = upper.reshape(NX // 2, NY // 2, NZ // 2, CO)
        grad_act = jnp.repeat(jnp.repeat(jnp.repeat(upper, 2, 0), 2, 1), 2, 2).astype(jnp.float32) * 0.125
        slope = jnp.where(before.reshape(NX, NY, NZ, CO) > 0, 1.0, 0.3).astype(jnp.float32)
        gate_grad = (grad_act * slope).astype(jnp.bfloat16)
        padded = jnp.pad(gate_grad, ((1, 1), (1, 1), (1, 1), (0, 0)))
        acts_flat = acts.reshape(-1, CI)
        input_acc = jnp.zeros((NX * NY * NZ, CI), jnp.float32)
        terms = []
        for index, offset in enumerate(stencil_offsets):
            ox, oy, oz = offset
            moved = padded[1 - ox:1 - ox + NX, 1 - oy:1 - oy + NY, 1 - oz:1 - oz + NZ, :].reshape(-1, CO)
            input_acc = input_acc + jnp.dot(moved, weights[index].T, preferred_element_type=jnp.float32)
            terms.append(jnp.dot(acts_flat.T, moved, preferred_element_type=jnp.float32))
        weight_acc = weight_acc + jnp.stack(terms, axis=0)
        bias_acc = bias_acc + jnp.sum(gate_grad.reshape(-1, CO).astype(jnp.float32), axis=0)
        return (weight_acc, bias_acc), input_acc.astype(jnp.bfloat16).reshape(NX, NY, NZ * CI)

    start = (jnp.zeros((27, CI, CO), jnp.float32), jnp.zeros((CO,), jnp.float32))
    (weight_acc, bias_acc), input_grad = lax.scan(per_sample, start, (activations, preact, pooled_grad))
    return input_grad, weight_acc / SAMPLES, bias_acc / SAMPLES
```

```python
import functools

import jax
import jax.numpy as jnp
from jax import lax
from jax.experimental import pallas as pl
from jax.experimental.pallas import tpu as pltpu
from jax.sharding import PartitionSpec as P

MESH = pl.DeviceIdType.MESH
AXES = ("dp", "sx", "sy")
ROWS = 8
LANES = 128
FACTORS = ("core", "chip", "sx", "sy")
CODE = 2.0**36
ONE_SHOT = 16
VMEM_LIMIT = 56 * 1024 * 1024


def span(name, sizes):
    pair = 2 if sizes[0] % 2 == 0 else 1
    return {"core": pair, "chip": sizes[0] // pair, "sx": sizes[1], "sy": sizes[2]}[name]


def plan_stages(sizes):
    rest = span("chip", sizes) * sizes[1] * sizes[2]
    groups = [("core",)]
    groups += [("chip", "sx", "sy")] if rest <= ONE_SHOT else [("chip",), ("sx",), ("sy",)]
    stages = []
    for group in groups:
        count = 1
        for name in group:
            count *= span(name, sizes)
        if count > 1:
            stages.append((group, count))
    return stages


def place():
    return tuple(lax.axis_index(axis) for axis in AXES)


def split(sizes, here):
    d, x, y = here
    pair = span("core", sizes)
    return {"core": d % pair, "chip": d // pair, "sx": x, "sy": y}


def member(sizes, group, here):
    values = split(sizes, here)
    index = 0
    for name in group:
        index = index * span(name, sizes) + values[name]
    return index


def peer(sizes, group, here, index):
    values = split(sizes, here)
    for name in reversed(group):
        values[name] = index % span(name, sizes)
        index = index // span(name, sizes)
    return (values["chip"] * span("core", sizes) + values["core"], values["sx"], values["sy"])


def encode(value):
    scaled = value * CODE
    return (scaled * jnp.abs(scaled)).astype(jnp.bfloat16)


def decode(coded):
    wide = coded.astype(jnp.float32)
    root = jnp.sqrt(jnp.abs(wide)) * (1.0 / CODE)
    return jnp.where(wide < 0, -root, root)


def body(sizes, stages, chunks, samples, acts_hbm, pre_hbm, pool_hbm, weights_hbm,
         grad_ref, wide_ref, bias_ref, *scratch):
    (acts_in, pre_in, pool_in, weights_ref, acts_wide, pre_wide, pool_wide, act_pl, gate_pl,
     far_pl, turned, taps, acc, total, landing, leaving, load_sem, halo_send, halo_recv,
     red_send, red_recv, gat_send, gat_recv) = scratch
    loads = [
        pltpu.make_async_copy(src, dst, load_sem.at[n])
        for n, (src, dst) in enumerate(
            ((acts_hbm, acts_in), (pre_hbm, pre_in), (pool_hbm, pool_in), (weights_hbm, weights_ref))
        )
    ]
    for load in loads:
        load.start()
    here = place()
    d, x, y = here
    cells_x = acts_in.shape[0]
    cells_y = act_pl.shape[0] - 2
    deep = act_pl.shape[2]
    offsets, chan_in, chan_out = weights_hbm.shape
    plane = cells_x * deep
    cells = cells_y * plane
    units = chan_in // ROWS
    bias_unit = offsets * units
    depth = len(stages)

    barrier = pltpu.get_barrier_semaphore()
    greeted = 0
    for group, count in stages:
        me = member(sizes, group, here)
        for turn in range(1, count):
            pl.semaphore_signal(
                barrier, inc=1, device_id=peer(sizes, group, here, (me + turn) % count),
                device_id_type=MESH,
            )
            greeted += 1
    one_shot = any(group == ("chip", "sx", "sy") for group, _ in stages)
    ways = [(0, -1), (0, 1), (-1, 0), (1, 0), (-1, -1), (-1, 1), (1, -1), (1, 1)]

    def inside(dx, dy):
        ok = None
        for coord, step, size in ((x, dx, sizes[1]), (y, dy, sizes[2])):
            if step == -1:
                term = coord > 0
            elif step == 1:
                term = coord < size - 1
            else:
                continue
            ok = term if ok is None else jnp.logical_and(ok, term)
        return ok

    if not one_shot:
        for dx, dy in ways:
            @pl.when(inside(dx, dy))
            def _():
                pl.semaphore_signal(
                    barrier, inc=1, device_id=(d, x + dx, y + dy), device_id_type=MESH
                )
        for dx, dy in ways:
            greeted = greeted + jnp.where(inside(dx, dy), 1, 0)

    def edge(step, size):
        return pl.ds(1, size) if step == 0 else (1 if step == -1 else size)

    def rim(step, size):
        return pl.ds(1, size) if step == 0 else (0 if step == -1 else size + 1)

    def halo_copy(kind, n, dx, dy):
        back = ways.index((-dx, -dy))
        if kind == 0:
            src = act_pl.at[edge(dy, cells_y), edge(dx, cells_x)]
            dst = act_pl.at[rim(-dy, cells_y), rim(-dx, cells_x)]
        else:
            src = gate_pl.at[:, edge(dy, cells_y), edge(dx, cells_x)]
            dst = gate_pl.at[:, rim(-dy, cells_y), rim(-dx, cells_x)]
        return pltpu.make_async_remote_copy(
            src_ref=src,
            dst_ref=dst,
            send_sem=halo_send.at[kind, n],
            recv_sem=halo_recv.at[kind, back],
            device_id=(d, x + dx, y + dy),
            device_id_type=MESH,
        )

    def arrived(kind, dx, dy):
        halo_copy(kind, ways.index((-dx, -dy)), -dx, -dy).wait_recv()

    def send_halo(kind):
        for n, (dx, dy) in enumerate(ways):
            @pl.when(inside(dx, dy))
            def _():
                halo_copy(kind, n, dx, dy).start()

    for dx, dy in ways:
        @pl.when(jnp.logical_not(inside(dx, dy)))
        def _():
            for ref in (
                act_pl.at[rim(dy, cells_y), rim(dx, cells_x)],
                gate_pl.at[:, rim(dy, cells_y), rim(dx, cells_x)],
            ):
                ref[...] = jnp.zeros(ref.shape, jnp.bfloat16)

    loads[0].wait()
    acts_wide[...] = acts_in[...].astype(jnp.float32).reshape(acts_wide.shape)
    for row in range(cells_y):
        act_pl[1 + row, pl.ds(1, cells_x)] = (
            acts_wide[pl.ds(row, plane, stride=cells_y), :]
            .astype(jnp.bfloat16)
            .reshape(cells_x, deep, LANES)
        )
    loads[1].wait()
    loads[2].wait()
    pre_wide[...] = pre_in[...].astype(jnp.float32).reshape(pre_wide.shape)
    pool_wide[...] = pool_in[...].astype(jnp.float32).reshape(pool_wide.shape) * 0.125
    bias = jnp.zeros((ROWS, chan_out), jnp.float32)
    slot = lax.broadcasted_iota(jnp.int32, (cells_x, deep, LANES), 1)
    for half in range(cells_y // 2):
        upper = pool_wide[pl.ds(half, plane // 2, stride=cells_y // 2), :]
        upper = jnp.broadcast_to(
            upper.reshape(cells_x // 2, 1, deep, LANES), (cells_x // 2, 2, deep, LANES)
        ).reshape(plane, LANES)
        for row in (2 * half, 2 * half + 1):
            for odd in (0, 1):
                before = pre_wide[pl.ds(odd * cells_y + row, plane, stride=2 * cells_y), :]
                gate = (upper * jnp.where(before > 0, 1.0, 0.3)).astype(jnp.bfloat16)
                wide = gate.astype(jnp.float32)
                bias = bias + jnp.sum(wide.reshape(-1, ROWS, chan_out), axis=0)
                wide = wide.reshape(cells_x, deep, LANES)
                gate_pl[odd, 1 + row, pl.ds(1, cells_x)] = gate.reshape(cells_x, deep, LANES)
                if odd:
                    away = jnp.where(slot == 0, 0.0, pltpu.roll(wide, 1, 1))
                else:
                    away = jnp.where(slot == deep - 1, 0.0, pltpu.roll(wide, deep - 1, 1))
                far_pl[odd, 1 + row, pl.ds(1, cells_x)] = away.astype(jnp.bfloat16)
    bias = jnp.sum(bias, axis=0, keepdims=True)
    top = lax.broadcasted_iota(jnp.int32, (ROWS, chan_out), 0) == 0
    acc[bias_unit] = jnp.where(top, jnp.broadcast_to(bias, (ROWS, chan_out)), 0.0)
    spare = acc.shape[0] - bias_unit - 1
    if spare:
        acc[pl.ds(bias_unit + 1, spare)] = jnp.zeros((spare, ROWS, chan_out), jnp.float32)

    pl.semaphore_wait(barrier, greeted)
    send_halo(0)
    send_halo(1)

    def turn_plane(a, row):
        piece = act_pl[row, pl.ds(1 + a, cells_x)].reshape(plane, LANES)
        turned[1 + a, :, pl.ds(row * plane, plane)] = piece.T

    inner = (pl.ds(1, cells_y), pl.ds(1, cells_x))

    def flat(ref, odd):
        return ref[odd, inner[0], inner[1]].reshape(cells, LANES)

    even = jnp.concatenate([flat(gate_pl, 1), flat(gate_pl, 0), flat(far_pl, 1)], axis=1)
    oddly = jnp.concatenate([flat(far_pl, 0), flat(gate_pl, 1), flat(gate_pl, 0)], axis=1)

    def weight_terms(a_first, a_count, b):
        span_b = pl.ds((1 + b) * plane, cells)
        rows = pl.ds(1 + a_first, a_count)
        lhs_even = turned[rows, pl.ds(0, chan_in), span_b].reshape(a_count * chan_in, cells)
        lhs_odd = turned[rows, pl.ds(chan_in, chan_in), span_b].reshape(a_count * chan_in, cells)
        term = jnp.dot(lhs_even, even, preferred_element_type=jnp.float32)
        term = term + jnp.dot(lhs_odd, oddly, preferred_element_type=jnp.float32)
        for n in range(a_count):
            first = 9 * (a_first + n + 1) + 3 * (b + 1)
            for c in range(3):
                acc[pl.ds((first + c) * units, units)] = term[
                    n * chan_in : (n + 1) * chan_in, c * chan_out : (c + 1) * chan_out
                ].reshape(units, ROWS, chan_out)

    for row in range(1, 1 + cells_y):
        turn_plane(0, row)
    weight_terms(0, 1, 0)
    for dx, dy in ways:
        @pl.when(inside(dx, dy))
        def _():
            arrived(0, dx, dy)
    for a in (-1, 0, 1):
        for row in range(cells_y + 2):
            if a or row in (0, cells_y + 1):
                turn_plane(a, row)
    weight_terms(-1, 1, 0)
    weight_terms(1, 1, 0)
    weight_terms(-1, 3, -1)
    weight_terms(-1, 3, 1)

    starts = [jnp.int32(0)]
    started = []

    def base_of(stage):
        return sum((stages[s][1] - 1) * chunks[s] for s in range(stage))

    def sem_of(stage, turn):
        return sum(count - 1 for _, count in stages[:stage]) + turn - 1

    def send_reduce(stage):
        group, count = stages[stage]
        chunk = chunks[stage]
        me = member(sizes, group, here)
        copies = []
        for turn in range(1, count):
            index = (me + turn) % count
            rows = pl.ds(base_of(stage) + (turn - 1) * chunk, chunk)
            leaving[rows] = encode(acc[pl.ds(starts[-1] + index * chunk, chunk)])
            copy = pltpu.make_async_remote_copy(
                src_ref=leaving.at[rows],
                dst_ref=landing.at[rows],
                send_sem=red_send.at[sem_of(stage, turn)],
                recv_sem=red_recv.at[sem_of(stage, turn)],
                device_id=peer(sizes, group, here, index),
                device_id_type=MESH,
            )
            copy.start()
            copies.append(copy)
            started.append(copy)
        return copies

    def take_reduce(stage, copies):
        group, count = stages[stage]
        chunk = chunks[stage]
        own = starts[-1] + member(sizes, group, here) * chunk
        value = acc[pl.ds(own, chunk)]
        for turn in range(1, count):
            copies[turn - 1].wait_recv()
            value = value + decode(landing[pl.ds(base_of(stage) + (turn - 1) * chunk, chunk)])
        acc[pl.ds(own, chunk)] = value
        starts.append(own)

    def make_taps():
        loads[3].wait()
        blank = jnp.zeros((chan_in, chan_out), jnp.bfloat16)
        for n in range(offsets // 3):
            three = [weights_ref[3 * n + c] for c in range(3)]
            taps[n, pl.ds(0, chan_in)] = jnp.concatenate([blank] + three, axis=1)
            taps[n, pl.ds(chan_in, chan_in)] = jnp.concatenate(three + [blank], axis=1)

    def fill_far():
        for dx, dy in ways:
            @pl.when(inside(dx, dy))
            def _():
                arrived(1, dx, dy)
        where = [(0, pl.ds(0, cells_x + 2)), (cells_y + 1, pl.ds(0, cells_x + 2))]
        where += [(1 + row, at) for row in range(cells_y) for at in (pl.ds(0, 1), pl.ds(cells_x + 1, 1))]
        for row, at in where:
            for odd in (0, 1):
                wide = gate_pl[odd, row, at].astype(jnp.float32)
                place_z = lax.broadcasted_iota(jnp.int32, wide.shape, 1)
                if odd:
                    away = jnp.where(place_z == 0, 0.0, pltpu.roll(wide, 1, 1))
                else:
                    away = jnp.where(place_z == deep - 1, 0.0, pltpu.roll(wide, deep - 1, 1))
                far_pl[odd, row, at] = away.astype(jnp.bfloat16)

    def input_gradient():
        sums = None
        for a in (-1, 0, 1):
            for b in (-1, 0, 1):
                ys, xs = pl.ds(1 - b, cells_y), pl.ds(1 - a, cells_x)
                lhs = jnp.concatenate(
                    [
                        ref[odd, ys, xs].reshape(cells, LANES)
                        for ref, odd in ((far_pl, 0), (gate_pl, 1), (gate_pl, 0), (far_pl, 1))
                    ],
                    axis=1,
                )
                term = lax.dot_general(
                    lhs,
                    taps[3 * (a + 1) + b + 1],
                    (((1,), (1,)), ((), ())),
                    preferred_element_type=jnp.float32,
                )
                sums = term if sums is None else sums + term
        for row in range(cells_y):
            acts_wide[pl.ds(row, plane, stride=cells_y), :] = sums[row * plane : (row + 1) * plane]
        grad_ref[...] = acts_wide[...].astype(jnp.bfloat16).reshape(grad_ref.shape)

    def pieces_of(stage):
        return stages[stage + 1][1] if stage + 1 < depth else 1

    def gather_copy(stage, turn, piece, where):
        group, count = stages[stage]
        slot = sum((stages[s][1] - 1) * pieces_of(s) for s in range(stage))
        slot += (turn - 1) * pieces_of(stage) + piece
        rows = pl.ds(where, chunks[min(stage + 1, depth - 1)])
        return pltpu.make_async_remote_copy(
            src_ref=total.at[rows],
            dst_ref=total.at[rows],
            send_sem=gat_send.at[slot],
            recv_sem=gat_recv.at[slot],
            device_id=peer(sizes, group, here, (member(sizes, group, here) + turn) % count),
            device_id_type=MESH,
        )

    def spread(stage, piece, where):
        for turn in range(1, stages[stage][1]):
            copy = gather_copy(stage, turn, piece, where)
            copy.start()
            started.append(copy)

    def unfold(where, size):
        rows = pl.ds(where, size)
        wide_ref[rows] = decode(total[rows])

    for stage in range(depth):
        copies = send_reduce(stage)
        if stage == 0:
            make_taps()
        if stage == depth - 1:
            fill_far()
            input_gradient()
        take_reduce(stage, copies)

    own, chunk = starts[-1], chunks[-1]
    value = acc[pl.ds(own, chunk)] * (1.0 / (samples * sizes[0]))
    coded = encode(value)
    rest = pltpu.roll(value - decode(coded), 1, 1)
    unit = own + lax.broadcasted_iota(jnp.int32, value.shape, 0)
    row = lax.broadcasted_iota(jnp.int32, value.shape, 1)
    is_rest = jnp.logical_and(unit == bias_unit, row == 1)
    total[pl.ds(own, chunk)] = encode(jnp.where(is_rest, rest, value))
    spread(depth - 1, 0, own)
    for stage in reversed(range(depth)):
        group, count = stages[stage]
        me = member(sizes, group, here)
        if stage:
            spread(stage - 1, 0, starts[stage + 1])
        if stage == depth - 1:
            unfold(own, chunk)
        for turn in range(1, count):
            first = starts[stage] + ((me - turn + count) % count) * chunks[stage]
            for piece in range(pieces_of(stage)):
                where, size = first, chunks[stage]
                if stage + 1 < depth:
                    size = chunks[stage + 1]
                    many = stages[stage + 1][1]
                    other = member(sizes, stages[stage + 1][0], here)
                    where = first + ((other - piece + many) % many) * size
                gather_copy(stage, turn, piece, where).wait_recv()
                unfold(where, size)
            if stage:
                spread(stage - 1, turn, first)
    bias_ref[...] = wide_ref[bias_unit, pl.ds(0, 1)] + wide_ref[bias_unit, pl.ds(1, 1)]
    for copy in started:
        copy.wait_send()
    for kind in (0, 1):
        for n, (dx, dy) in enumerate(ways):
            @pl.when(inside(dx, dy))
            def _():
                halo_copy(kind, n, dx, dy).wait_send()


def fused(acts, before, upper, weights, cells_y, samples, sizes):
    cells_x, rows_acts, _ = acts.shape
    deep = rows_acts // cells_y
    offsets, chan_in, chan_out = weights.shape
    stages = plan_stages(sizes)
    devices = 1
    for _, count in stages:
        devices *= count
    units = -(-(offsets * chan_in // ROWS + 1) // devices) * devices
    chunks = []
    for _, count in stages:
        chunks.append((chunks[-1] if chunks else units) // count)
    moved = sum((count - 1) * chunk for (_, count), chunk in zip(stages, chunks))
    hops = sum(count - 1 for _, count in stages)
    pieces = [count for _, count in stages[1:]] + [1]
    parts = sum((count - 1) * piece for (_, count), piece in zip(stages, pieces))
    half, full = jnp.bfloat16, jnp.float32
    padded = (cells_y + 2, cells_x + 2, deep, LANES)
    cells = cells_x * rows_acts
    scratch = [
        pltpu.VMEM(acts.shape, half),
        pltpu.VMEM(before.shape, half),
        pltpu.VMEM(upper.shape, half),
        pltpu.VMEM(weights.shape, half),
        pltpu.VMEM((cells, LANES), full),
        pltpu.VMEM((2 * cells, LANES), full),
        pltpu.VMEM((upper.shape[0] * upper.shape[1], LANES), full),
        pltpu.VMEM(padded, half),
        pltpu.VMEM((2,) + padded, half),
        pltpu.VMEM((2,) + padded, half),
        pltpu.VMEM((3, LANES, (cells_y + 2) * cells_x * deep), half),
        pltpu.VMEM((offsets // 3, LANES, 4 * chan_out), half),
        pltpu.VMEM((units, ROWS, chan_out), full),
        pltpu.VMEM((units, ROWS, chan_out), half),
        pltpu.VMEM((moved, ROWS, chan_out), half),
        pltpu.VMEM((moved, ROWS, chan_out), half),
        pltpu.SemaphoreType.DMA((4,)),
        pltpu.SemaphoreType.DMA((2, 8)),
        pltpu.SemaphoreType.DMA((2, 8)),
        pltpu.SemaphoreType.DMA((hops,)),
        pltpu.SemaphoreType.DMA((hops,)),
        pltpu.SemaphoreType.DMA((parts,)),
        pltpu.SemaphoreType.DMA((parts,)),
    ]
    return pl.pallas_call(
        functools.partial(body, sizes, stages, chunks, samples),
        out_shape=(
            jax.ShapeDtypeStruct(acts.shape, half),
            jax.ShapeDtypeStruct((units, ROWS, chan_out), full),
            jax.ShapeDtypeStruct((1, chan_out), full),
        ),
        in_specs=[pl.BlockSpec(memory_space=pltpu.MemorySpace.HBM)] * 4,
        out_specs=(pl.BlockSpec(memory_space=pltpu.VMEM),) * 3,
        scratch_shapes=scratch,
        compiler_params=pltpu.CompilerParams(
            collective_id=0, has_side_effects=True, vmem_limit_bytes=VMEM_LIMIT
        ),
    )(acts, before, upper, weights)


def fold(array):
    rows, cols, flat = array.shape
    array = array.reshape(rows, cols, flat // LANES, LANES).transpose(0, 2, 1, 3)
    return array.reshape(rows, flat // LANES * cols, LANES)


def on_device(sizes, activations, preact, pooled_grad, weights):
    samples, cells_x, cells_y, _ = activations.shape
    offsets, chan_in, chan_out = weights.shape
    acts = fold(activations.reshape(activations.shape[1:]))
    before = fold(preact.reshape(preact.shape[1:]))
    upper = fold(pooled_grad.reshape(pooled_grad.shape[1:]))
    grad, total, bias = fused(acts, before, upper, weights, cells_y, samples, sizes)
    grad = grad.reshape(cells_x, -1, cells_y, LANES).transpose(0, 2, 1, 3)
    unit = offsets * chan_in // ROWS
    return (
        grad.reshape(activations.shape),
        total[:unit].reshape(offsets, chan_in, chan_out),
        bias.reshape(chan_out),
    )


def solution(mesh):
    sizes = tuple(mesh.shape[axis] for axis in AXES)
    placed = (P("dp", "sx", "sy", None), P("dp", "sx", "sy", None), P("dp", "sx", "sy", None), P())
    return jax.shard_map(
        functools.partial(on_device, sizes),
        mesh=mesh,
        in_specs=placed,
        out_specs=(P("dp", "sx", "sy", None), P(), P()),
        check_vma=False,
    )
```

```python
import functools
import math

import jax
import jax.numpy as jnp
from jax import lax
from jax.experimental import pallas as pl
from jax.experimental.pallas import tpu as pltpu
from jax.sharding import PartitionSpec as P

MESH = pl.DeviceIdType.MESH
AXES = ("dp", "sx", "sy")
ROWS = 8
LANES = 128
FACTORS = ("core", "chip", "sx", "sy")
CODE = 2.0**36
ONE_SHOT = 16
PARTS = 3
VMEM_LIMIT = 56 * 1024 * 1024
STORE_LIMIT = 8 * 1024 * 1024


def span(name, sizes):
    pair = 2 if sizes[0] % 2 == 0 else 1
    return {"core": pair, "chip": sizes[0] // pair, "sx": sizes[1], "sy": sizes[2]}[name]


def plan_stages(sizes):
    rest = span("chip", sizes) * sizes[1] * sizes[2]
    groups = [("chip", "sx", "sy")] if rest <= ONE_SHOT else [("chip",), ("sx",), ("sy",)]
    stages = []
    for group in groups:
        count = 1
        for name in group:
            count *= span(name, sizes)
        if count > 1:
            stages.append((group, count))
    return stages


def near_first(sizes, group):
    def steps(index):
        total = 0
        for name in reversed(group):
            total += index % span(name, sizes)
            index //= span(name, sizes)
        return total

    count = 1
    for name in group:
        count *= span(name, sizes)
    return sorted(range(count), key=lambda index: (steps(index), index))


def place():
    return tuple(lax.axis_index(axis) for axis in AXES)


def split(sizes, here):
    d, x, y = here
    pair = span("core", sizes)
    return {"core": d % pair, "chip": d // pair, "sx": x, "sy": y}


def member(sizes, group, here):
    values = split(sizes, here)
    index = 0
    for name in group:
        index = index * span(name, sizes) + values[name]
    return index


def peer(sizes, group, here, index):
    values = split(sizes, here)
    for name in reversed(group):
        values[name] = index % span(name, sizes)
        index = index // span(name, sizes)
    return (values["chip"] * span("core", sizes) + values["core"], values["sx"], values["sy"])


def encode(value):
    scaled = value * CODE
    return (scaled * jnp.abs(scaled)).astype(jnp.bfloat16)


def decode(coded):
    wide = coded.astype(jnp.float32)
    root = jnp.sqrt(jnp.abs(wide)) * (1.0 / CODE)
    return jnp.where(wide < 0, -root, root)


def body(sizes, stages, chunks, samples, acts_hbm, pre_hbm, pool_hbm, weights_hbm,
         grad_ref, wide_ref, bias_ref, *scratch):
    (acts_in, pre_in, pool_in, weights_ref, acts_wide, pre_wide, pool_wide, planes, far,
     turned, taps, acc, total, landing, leaving, load_sem, halo_send, halo_recv,
     pair_send, pair_recv, red_send, red_recv, gat_send, gat_recv, fwd_send, fwd_recv) = scratch
    loads = [
        pltpu.make_async_copy(src, dst, load_sem.at[n])
        for n, (src, dst) in enumerate(
            ((acts_hbm, acts_in), (pre_hbm, pre_in), (pool_hbm, pool_in), (weights_hbm, weights_ref))
        )
    ]
    for load in loads[:3]:
        load.start()
    here = place()
    d, x, y = here
    pair = span("core", sizes)
    core = d % pair
    mate = d + 1 - 2 * core if pair == 2 else d
    cells_x = acts_in.shape[0]
    cells_y, deep = planes.shape[2] - 2, planes.shape[4]
    offsets, chan_in, chan_out = weights_hbm.shape
    share = chan_in // pair
    plane = cells_x * deep
    cells = cells_y * plane
    units = share // ROWS
    bias_unit = offsets * units
    depth = len(stages)
    ways = [(0, -1), (0, 1), (-1, 0), (1, 0), (-1, -1), (-1, 1), (1, -1), (1, 1)]

    def inside(dx, dy):
        ok = None
        for coord, step, size in ((x, dx, sizes[1]), (y, dy, sizes[2])):
            if step == -1:
                term = coord > 0
            elif step == 1:
                term = coord < size - 1
            else:
                continue
            ok = term if ok is None else jnp.logical_and(ok, term)
        return ok

    barrier = pltpu.get_barrier_semaphore()
    greeted = 0

    def greet(target):
        pl.semaphore_signal(barrier, inc=1, device_id=target, device_id_type=MESH)

    if pair == 2:
        greet((mate, x, y))
        greeted += 1
    for group, count in stages:
        me = member(sizes, group, here)
        for turn in range(1, count):
            greet(peer(sizes, group, here, (me + turn) % count))
            greeted += 1
    known = any(group == ("chip", "sx", "sy") for group, _ in stages)
    for dx, dy in ways:
        @pl.when(inside(dx, dy))
        def _():
            if pair == 2:
                greet((mate, x + dx, y + dy))
            if not known:
                greet((d, x + dx, y + dy))
    for dx, dy in ways:
        greeted = greeted + jnp.where(inside(dx, dy), pair - 1 + (0 if known else 1), 0)

    def edge(step, size):
        return pl.ds(1, size) if step == 0 else (1 if step == -1 else size)

    def rim(step, size):
        return pl.ds(1, size) if step == 0 else (0 if step == -1 else size + 1)

    def halo_copy(kind, slot, dx, dy):
        kinds = 0 if kind == 0 else pl.ds(1, 2)
        return pltpu.make_async_remote_copy(
            src_ref=planes.at[0, kinds, edge(dy, cells_y), edge(dx, cells_x)],
            dst_ref=planes.at[slot, kinds, rim(-dy, cells_y), rim(-dx, cells_x)],
            send_sem=halo_send.at[ways.index((dx, dy))],
            recv_sem=halo_recv.at[kind, ways.index((-dx, -dy))],
            device_id=(mate if slot else d, x + dx, y + dy),
            device_id_type=MESH,
        )

    def whole(ref, send_sem, recv_sem):
        return pltpu.make_async_remote_copy(
            src_ref=ref, dst_ref=ref, send_sem=send_sem, recv_sem=recv_sem,
            device_id=(mate, x, y), device_id_type=MESH,
        )

    def halo_arrived(kind):
        for n, (dx, dy) in enumerate(ways):
            @pl.when(inside(dx, dy))
            def _():
                where = (rim(dy, cells_y), rim(dx, cells_x))
                ref = planes.at[:, 0, *where] if kind == 0 else planes.at[0, pl.ds(1, 2), *where]
                whole(ref, halo_send.at[n], halo_recv.at[kind, n]).wait_recv()

    def halo_left():
        for n, (dx, dy) in enumerate(ways):
            @pl.when(inside(dx, dy))
            def _():
                where = (edge(dy, cells_y), edge(dx, cells_x))
                ref = planes.at[:, pl.ds(0, 2), *where] if pair == 2 else planes.at[0, :, *where]
                whole(ref, halo_send.at[n], halo_recv.at[0, n]).wait_send()

    def send_halo(kind):
        for dx, dy in ways:
            @pl.when(inside(dx, dy))
            def _():
                halo_copy(kind, 0, dx, dy).start()
                if kind == 0 and pair == 2:
                    halo_copy(kind, 1, dx, dy).start()

    inner = (pl.ds(1, cells_y), pl.ds(1, cells_x))

    def pair_copy(kind):
        kinds = pl.ds(0, 1) if kind == 0 else pl.ds(1, 2)
        return pltpu.make_async_remote_copy(
            src_ref=planes.at[0, kinds, *inner],
            dst_ref=planes.at[1, kinds, *inner],
            send_sem=pair_send.at[0],
            recv_sem=pair_recv.at[kind],
            device_id=(mate, x, y),
            device_id_type=MESH,
        )

    for dx, dy in ways:
        @pl.when(jnp.logical_not(inside(dx, dy)))
        def _():
            where = (rim(dy, cells_y), rim(dx, cells_x))
            for ref in [planes.at[0, n, *where] for n in range(3)] + [
                planes.at[slot, 0, *where] for slot in range(1, pair)
            ]:
                ref[...] = jnp.zeros(ref.shape, jnp.bfloat16)

    loads[0].wait()
    acts_wide[...] = acts_in[...].astype(jnp.float32).reshape(acts_wide.shape)
    for row in range(cells_y):
        planes[0, 0, 1 + row, pl.ds(1, cells_x)] = (
            acts_wide[pl.ds(row, plane, stride=cells_y), :]
            .astype(jnp.bfloat16)
            .reshape(cells_x, deep, LANES)
        )
    pl.semaphore_wait(barrier, greeted)
    send_halo(0)
    if pair == 2:
        pair_copy(0).start()
    loads[1].wait()
    loads[2].wait()
    loads[3].start()
    pre_wide[...] = pre_in[...].astype(jnp.float32).reshape(pre_wide.shape)
    pool_wide[...] = pool_in[...].astype(jnp.float32).reshape(pool_wide.shape) * 0.125
    for half in range(cells_y // 2):
        upper = pool_wide[pl.ds(half, plane // 2, stride=cells_y // 2), :]
        upper = jnp.broadcast_to(
            upper.reshape(cells_x // 2, 1, deep, LANES), (cells_x // 2, 2, deep, LANES)
        ).reshape(plane, LANES)
        for row in (2 * half, 2 * half + 1):
            for odd in (0, 1):
                before = pre_wide[pl.ds(odd * cells_y + row, plane, stride=2 * cells_y), :]
                gate = (upper * jnp.where(before > 0, 1.0, 0.3)).astype(jnp.bfloat16)
                planes[0, 1 + odd, 1 + row, pl.ds(1, cells_x)] = gate.reshape(cells_x, deep, LANES)
    if pair == 2:
        pair_copy(1).start()
    send_halo(1)

    def shift_z(slot, odd, rows, cols):
        wide = planes[slot, 1 + odd, rows, cols].astype(jnp.float32)
        axis = wide.ndim - 2
        depth_z = lax.broadcasted_iota(jnp.int32, wide.shape, axis)
        if odd:
            moved = jnp.where(depth_z == 0, 0.0, pltpu.roll(wide, 1, axis))
        else:
            moved = jnp.where(depth_z == deep - 1, 0.0, pltpu.roll(wide, deep - 1, axis))
        far[slot, odd, rows, cols] = moved.astype(jnp.bfloat16)

    def turn_planes(slot, rows, a_all):
        for row in rows:
            for a in a_all:
                piece = planes[slot, 0, row, pl.ds(1 + a, cells_x)].reshape(plane, LANES)
                turned[slot, 1 + a, :, pl.ds(row * plane, plane)] = piece.T

    bias = jnp.zeros((ROWS, chan_out), jnp.float32)
    middle = range(1, 1 + cells_y)
    for slot in range(pair):
        if slot:
            for kind in (0, 1):
                pair_copy(kind).wait_recv()
        for odd in (0, 1):
            for row in middle:
                shift_z(slot, odd, row, pl.ds(1, cells_x))
                wide = planes[slot, 1 + odd, row, pl.ds(1, cells_x)].astype(jnp.float32)
                bias = bias + jnp.sum(wide.reshape(-1, ROWS, chan_out), axis=0)
        turn_planes(slot, middle, (0,))
    bias = jnp.sum(bias, axis=0, keepdims=True)
    top = lax.broadcasted_iota(jnp.int32, (ROWS, chan_out), 0) == 0
    acc[bias_unit] = jnp.where(top, jnp.broadcast_to(bias, (ROWS, chan_out)), 0.0)
    spare = acc.shape[0] - bias_unit - 1
    if spare:
        acc[pl.ds(bias_unit + 1, spare)] = jnp.zeros((spare, ROWS, chan_out), jnp.float32)

    halo_arrived(0)
    for slot in range(pair):
        turn_planes(slot, range(cells_y + 2), (-1, 1))
        turn_planes(slot, (0, cells_y + 1), (0,))

    def flat(ref, slot, odd):
        return ref[slot, odd, inner[0], inner[1]].reshape(cells, LANES)

    term = None
    for slot in range(pair):
        for odd in (0, 1):
            if odd:
                kinds = ((far, 0), (planes, 2), (planes, 1))
            else:
                kinds = ((planes, 2), (planes, 1), (far, 1))
            rhs = jnp.concatenate([flat(ref, slot, n) for ref, n in kinds], axis=1)
            rows = pl.ds(pl.multiple_of(odd * chan_in + core * share, share), share)
            lhs = jnp.concatenate(
                [
                    turned[slot, a, rows, pl.ds(b * plane, cells)]
                    for a in range(3)
                    for b in range(3)
                ],
                axis=0,
            )
            piece = jnp.dot(lhs, rhs, preferred_element_type=jnp.float32)
            term = piece if term is None else term + piece
    for n in range(offsets // 3):
        for c in range(3):
            acc[pl.ds((3 * n + c) * units, units)] = term[
                n * share : (n + 1) * share, c * chan_out : (c + 1) * chan_out
            ].reshape(units, ROWS, chan_out)

    starts = [0]

    def span_of(stage, index):
        return pl.ds(starts[stage] + index * chunks[stage], chunks[stage])

    def offset_of(stage):
        return sum((stages[s][1] - 1) * chunks[s] for s in range(stage))

    def arrivals(stage):
        return pl.ds(offset_of(stage), (stages[stage][1] - 1) * chunks[stage])

    def send_reduce(stage):
        group, count = stages[stage]
        chunk = chunks[stage]
        me = member(sizes, group, here)
        rows = pl.ds(starts[stage], count * chunk)
        leaving[rows] = encode(acc[rows])
        for index in near_first(sizes, group):
            @pl.when(me != index)
            def _():
                slot = (me - index + count) % count - 1
                pltpu.make_async_remote_copy(
                    src_ref=leaving.at[span_of(stage, index)],
                    dst_ref=landing.at[pl.ds(offset_of(stage) + slot * chunk, chunk)],
                    send_sem=red_send.at[stage],
                    recv_sem=red_recv.at[stage],
                    device_id=peer(sizes, group, here, index),
                    device_id_type=MESH,
                ).start()

    def take_reduce(stage):
        group, count = stages[stage]
        chunk = chunks[stage]
        own = starts[stage] + member(sizes, group, here) * chunk
        ref = landing.at[arrivals(stage)]
        copies = whole(ref, red_send.at[stage], red_recv.at[stage])
        copies.wait_recv()
        value = acc[pl.ds(own, chunk)]
        for turn in range(count - 1):
            value = value + decode(landing[pl.ds(offset_of(stage) + turn * chunk, chunk)])
        copies.wait_send()
        acc[pl.ds(own, chunk)] = value
        starts.append(own)

    def make_taps():
        loads[3].wait()
        blank = jnp.zeros((chan_in, chan_out), jnp.bfloat16)
        for n in range(offsets // 3):
            three = [weights_ref[3 * n + c] for c in range(3)]
            taps[n, pl.ds(0, chan_in)] = jnp.concatenate([blank] + three, axis=1)
            taps[n, pl.ds(chan_in, chan_in)] = jnp.concatenate(three + [blank], axis=1)

    def input_gradient():
        make_taps()
        halo_arrived(1)
        for odd in (0, 1):
            for row in (0, cells_y + 1):
                shift_z(0, odd, row, pl.ds(0, cells_x + 2))
            for col in (0, cells_x + 1):
                shift_z(0, odd, pl.ds(1, cells_y), col)
        sums = None
        for a in (-1, 0, 1):
            for b in (-1, 0, 1):
                ys, xs = pl.ds(1 - b, cells_y), pl.ds(1 - a, cells_x)
                lhs = jnp.concatenate(
                    [
                        ref[0, n, ys, xs].reshape(cells, LANES)
                        for ref, n in ((far, 0), (planes, 2), (planes, 1), (far, 1))
                    ],
                    axis=1,
                )
                piece = lax.dot_general(
                    lhs,
                    taps[3 * (a + 1) + b + 1],
                    (((1,), (1,)), ((), ())),
                    preferred_element_type=jnp.float32,
                )
                sums = piece if sums is None else sums + piece
        for row in range(cells_y):
            acts_wide[pl.ds(row, plane, stride=cells_y), :] = sums[row * plane : (row + 1) * plane]
        grad_ref[...] = acts_wide[...].astype(jnp.bfloat16).reshape(grad_ref.shape)

    for stage in range(depth):
        send_reduce(stage)
        if stage == 0:
            input_gradient()
        take_reduce(stage)

    own, chunk = starts[-1], chunks[-1]
    value = acc[pl.ds(own, chunk)] * (1.0 / (samples * sizes[0]))
    coded = encode(value)
    rest = pltpu.roll(value - decode(coded), 1, 1)
    unit = own + lax.broadcasted_iota(jnp.int32, value.shape, 0)
    row = lax.broadcasted_iota(jnp.int32, value.shape, 1)
    is_rest = jnp.logical_and(unit == bias_unit, row == 1)
    total[core, pl.ds(own, chunk)] = encode(jnp.where(is_rest, rest, value))

    def parts_of(count):
        return -(-(count - 1) // PARTS)

    def unfold(side, rows):
        wide_ref[side, rows] = decode(total[side, rows])

    def forward(part, rows):
        ref = total.at[core, rows]
        pltpu.make_async_remote_copy(
            src_ref=ref, dst_ref=ref, send_sem=fwd_send.at[0], recv_sem=fwd_recv.at[part],
            device_id=(mate, x, y), device_id_type=MESH,
        ).start()

    for stage in reversed(range(depth)):
        group, count = stages[stage]
        me = member(sizes, group, here)
        size = parts_of(count)
        ref = total.at[core, span_of(stage, me)]
        for index in near_first(sizes, group):
            @pl.when(me != index)
            def _():
                part = stage * PARTS + ((me - index + count) % count - 1) // size
                pltpu.make_async_remote_copy(
                    src_ref=ref, dst_ref=ref, send_sem=gat_send.at[stage],
                    recv_sem=gat_recv.at[part],
                    device_id=peer(sizes, group, here, index), device_id_type=MESH,
                ).start()
        last = stage == 0
        if last and pair == 2:
            forward(0, span_of(stage, me))
        if stage == depth - 1:
            unfold(core, span_of(stage, me))
        for part in range(PARTS):
            turns = range(1 + part * size, min(1 + (part + 1) * size, count))
            if not turns:
                continue
            ref = total.at[0, pl.ds(0, len(turns) * chunks[stage])]
            whole(ref, gat_send.at[stage], gat_recv.at[stage * PARTS + part]).wait_recv()
            if last and pair == 2:
                for turn in turns:
                    forward(1 + part, span_of(stage, (me + turn) % count))
            for turn in turns:
                unfold(core, span_of(stage, (me + turn) % count))
    group, count = stages[0]
    me = member(sizes, group, here)
    size = parts_of(count)
    if pair == 2:
        for part in range(PARTS + 1):
            turns = [0] if part == 0 else range(1 + (part - 1) * size, min(1 + part * size, count))
            if not turns:
                continue
            ref = total.at[0, pl.ds(0, len(turns) * chunks[0])]
            whole(ref, fwd_send.at[0], fwd_recv.at[part]).wait_recv()
            for turn in turns:
                unfold(1 - core, span_of(0, (me + turn) % count))
    bias_ref[...] = wide_ref[0, bias_unit, pl.ds(0, 1)] + wide_ref[0, bias_unit, pl.ds(1, 1)]
    for stage in range(depth):
        ref = total.at[0, pl.ds(0, (stages[stage][1] - 1) * chunks[stage])]
        whole(ref, gat_send.at[stage], gat_recv.at[stage * PARTS]).wait_send()
    if pair == 2:
        whole(total.at[0], fwd_send.at[0], fwd_recv.at[0]).wait_send()
        ref = planes.at[0, :, *inner]
        whole(ref, pair_send.at[0], pair_recv.at[0]).wait_send()
    halo_left()


def fused(acts, before, upper, weights, cells_y, samples, sizes):
    cells_x, rows_acts, _ = acts.shape
    deep = rows_acts // cells_y
    offsets, chan_in, chan_out = weights.shape
    stages = plan_stages(sizes)
    pair = span("core", sizes)
    devices = 1
    for _, count in stages:
        devices *= count
    per_tap = chan_in // pair // ROWS
    step = math.lcm(devices, per_tap)
    units = -(-(offsets * per_tap + 1) // step) * step
    chunks = []
    for _, count in stages:
        chunks.append((chunks[-1] if chunks else units) // count)
    moved = sum((count - 1) * chunk for (_, count), chunk in zip(stages, chunks))
    half, full = jnp.bfloat16, jnp.float32
    padded = (cells_y + 2, cells_x + 2, deep, LANES)
    cells = cells_x * rows_acts
    dma = pltpu.SemaphoreType.DMA
    scratch = [
        pltpu.VMEM(acts.shape, half),
        pltpu.VMEM(before.shape, half),
        pltpu.VMEM(upper.shape, half),
        pltpu.VMEM(weights.shape, half),
        pltpu.VMEM((cells, LANES), full),
        pltpu.VMEM((2 * cells, LANES), full),
        pltpu.VMEM((upper.shape[0] * upper.shape[1], LANES), full),
        pltpu.VMEM((pair, 3) + padded, half),
        pltpu.VMEM((pair, 2) + padded, half),
        pltpu.VMEM((pair, 3, LANES, (cells_y + 2) * cells_x * deep), half),
        pltpu.VMEM((offsets // 3, LANES, 4 * chan_out), half),
        pltpu.VMEM((units, ROWS, chan_out), full),
        pltpu.VMEM((pair, units, ROWS, chan_out), half),
        pltpu.VMEM((moved, ROWS, chan_out), half),
        pltpu.VMEM((units, ROWS, chan_out), half),
        dma((4,)),
        dma((8,)),
        dma((2, 8)),
        dma((1,)),
        dma((2,)),
        dma((len(stages),)),
        dma((len(stages),)),
        dma((len(stages),)),
        dma((len(stages) * PARTS,)),
        dma((1,)),
        dma((PARTS + 1,)),
    ]
    return pl.pallas_call(
        functools.partial(body, sizes, stages, chunks, samples),
        out_shape=(
            pltpu.VMEM(acts.shape, half),
            pltpu.VMEM((pair, units, ROWS, chan_out), full),
            pltpu.VMEM((1, chan_out), full),
        ),
        in_specs=[pl.BlockSpec(memory_space=pltpu.MemorySpace.HBM)] * 4,
        out_specs=(pl.BlockSpec(memory_space=pltpu.VMEM),) * 3,
        scratch_shapes=scratch,
        compiler_params=pltpu.CompilerParams(
            collective_id=0, has_side_effects=True, vmem_limit_bytes=VMEM_LIMIT
        ),
    )(acts, before, upper, weights)


def store(grad_in, wide_in, bias_in, grad_out, wide_out, bias_out, sems):
    pair, _, share, _ = wide_in.shape
    copies = [
        pltpu.make_async_copy(
            wide_in.at[side, pl.ds(0, wide_out.shape[0])],
            wide_out.at[:, pl.ds(side * share, share)],
            sems.at[2 + side],
        )
        for side in range(pair)
    ]
    copies.append(pltpu.make_async_copy(grad_in, grad_out, sems.at[0]))
    copies.append(pltpu.make_async_copy(bias_in, bias_out, sems.at[1]))
    for copy in copies:
        copy.start()
    for copy in copies:
        copy.wait()


def finish(grad, wide, bias, offsets):
    pair, _, share, chan_out = wide.shape
    return pl.pallas_call(
        store,
        out_shape=(
            jax.ShapeDtypeStruct(grad.shape, grad.dtype),
            jax.ShapeDtypeStruct((offsets, pair * share, chan_out), wide.dtype),
            jax.ShapeDtypeStruct(bias.shape, bias.dtype),
        ),
        in_specs=[pl.BlockSpec(memory_space=pltpu.VMEM)] * 3,
        out_specs=(pl.BlockSpec(memory_space=pltpu.MemorySpace.HBM),) * 3,
        scratch_shapes=[pltpu.SemaphoreType.DMA((2 + pair,))],
        compiler_params=pltpu.CompilerParams(vmem_limit_bytes=STORE_LIMIT),
    )(grad, wide, bias)


def fold(array):
    rows, cols, flat = array.shape
    array = array.reshape(rows, cols, flat // LANES, LANES).transpose(0, 2, 1, 3)
    return array.reshape(rows, flat // LANES * cols, LANES)


def on_device(sizes, activations, preact, pooled_grad, weights):
    samples, cells_x, cells_y, _ = activations.shape
    offsets, chan_in, chan_out = weights.shape
    acts = fold(activations.reshape(activations.shape[1:]))
    before = fold(preact.reshape(preact.shape[1:]))
    upper = fold(pooled_grad.reshape(pooled_grad.shape[1:]))
    grad, total, bias = fused(acts, before, upper, weights, cells_y, samples, sizes)
    pair = span("core", sizes)
    total = total.reshape(pair, -1, chan_in // pair, chan_out)
    grad, total, bias = finish(grad, total, bias, offsets)
    grad = grad.reshape(cells_x, -1, cells_y, LANES).transpose(0, 2, 1, 3)
    return (
        grad.reshape(activations.shape),
        total,
        bias.reshape(chan_out),
    )


def solution(mesh):
    sizes = tuple(mesh.shape[axis] for axis in AXES)
    placed = (P("dp", "sx", "sy", None), P("dp", "sx", "sy", None), P("dp", "sx", "sy", None), P())
    return jax.shard_map(
        functools.partial(on_device, sizes),
        mesh=mesh,
        in_specs=placed,
        out_specs=(P("dp", "sx", "sy", None), P(), P()),
        check_vma=False,
    )
```

```python
import functools
import math

import jax
import jax.numpy as jnp
from jax import lax
from jax.experimental import pallas as pl
from jax.experimental.pallas import tpu as pltpu
from jax.sharding import PartitionSpec as P

MESH = pl.DeviceIdType.MESH
AXES = ("dp", "sx", "sy")
ROWS = 8
LANES = 128
FACTORS = ("core", "chip", "sx", "sy")
CODE = 2.0**36
ONE_SHOT = 16
PARTS = 5
BACK = 1
FIRST = 1
REDUCE_WAY = -1
GATHER_WAY = -1
VMEM_LIMIT = 56 * 1024 * 1024
STORE_LIMIT = 8 * 1024 * 1024


def span(name, sizes):
    pair = 2 if sizes[0] % 2 == 0 else 1
    return {"core": pair, "chip": sizes[0] // pair, "sx": sizes[1], "sy": sizes[2]}[name]


def plan_stages(sizes):
    rest = span("chip", sizes) * sizes[1] * sizes[2]
    groups = [("chip", "sx", "sy")] if rest <= ONE_SHOT else [("chip",), ("sx",), ("sy",)]
    stages = []
    for group in groups:
        count = 1
        for name in group:
            count *= span(name, sizes)
        if count > 1:
            stages.append((group, count))
    return stages


def digits(sizes, group):
    found = []
    for name in group:
        left = span(name, sizes)
        while left % 2 == 0:
            found.append(2)
            left //= 2
        if left > 1:
            found.append(left)
    return found


def moved(radices, index, move, way=1):
    result, weight = 0, 1
    for radix in reversed(radices):
        result = result + (index % radix + way * (move % radix) + radix) % radix * weight
        index, move, weight = index // radix, move // radix, weight * radix
    return result


def moves_of(sizes, group, way):
    count = 1
    for name in group:
        count *= span(name, sizes)

    def steps(move):
        total = 0
        for name in reversed(group):
            size = span(name, sizes)
            total += move % size
            move //= size
        return way * total

    return sorted(range(1, count), key=steps)


def place():
    return tuple(lax.axis_index(axis) for axis in AXES)


def split(sizes, here):
    d, x, y = here
    pair = span("core", sizes)
    return {"core": d % pair, "chip": d // pair, "sx": x, "sy": y}


def member(sizes, group, here):
    values = split(sizes, here)
    index = 0
    for name in group:
        index = index * span(name, sizes) + values[name]
    return index


def peer(sizes, group, here, index):
    values = split(sizes, here)
    for name in reversed(group):
        values[name] = index % span(name, sizes)
        index = index // span(name, sizes)
    return (values["chip"] * span("core", sizes) + values["core"], values["sx"], values["sy"])


def encode(value):
    scaled = value * CODE
    return (scaled * jnp.abs(scaled)).astype(jnp.bfloat16)


def decode(coded):
    wide = coded.astype(jnp.float32)
    root = jnp.sqrt(jnp.abs(wide)) * (1.0 / CODE)
    return jnp.where(wide < 0, -root, root)


def body(sizes, stages, chunks, samples, acts_hbm, pre_hbm, pool_hbm, weights_hbm,
         grad_ref, wide_ref, bias_ref, *scratch):
    (acts_in, pre_in, pool_in, weights_ref, acts_wide, pre_wide, pool_wide, planes, far,
     turned, taps, acc, total, landing, leaving, load_sem, halo_send, halo_recv,
     pair_send, pair_recv, red_send, red_recv, gat_send, gat_recv, fwd_send, fwd_recv) = scratch
    loads = [
        pltpu.make_async_copy(src, dst, load_sem.at[n])
        for n, (src, dst) in enumerate(
            ((acts_hbm, acts_in), (pre_hbm, pre_in), (pool_hbm, pool_in), (weights_hbm, weights_ref))
        )
    ]
    for load in loads[:3]:
        load.start()
    here = place()
    d, x, y = here
    pair = span("core", sizes)
    core = d % pair
    mate = d + 1 - 2 * core if pair == 2 else d
    cells_x = acts_in.shape[0]
    cells_y, deep = planes.shape[2] - 2, planes.shape[4]
    offsets, chan_in, chan_out = weights_hbm.shape
    share = chan_in // pair
    plane = cells_x * deep
    cells = cells_y * plane
    units = share // ROWS
    bias_unit = offsets * units
    depth = len(stages)
    ways = [(0, -1), (0, 1), (-1, 0), (1, 0), (-1, -1), (-1, 1), (1, -1), (1, 1)]

    def inside(dx, dy):
        ok = None
        for coord, step, size in ((x, dx, sizes[1]), (y, dy, sizes[2])):
            if step == -1:
                term = coord > 0
            elif step == 1:
                term = coord < size - 1
            else:
                continue
            ok = term if ok is None else jnp.logical_and(ok, term)
        return ok

    barrier = pltpu.get_barrier_semaphore()
    greeted = 0

    def greet(target):
        pl.semaphore_signal(barrier, inc=1, device_id=target, device_id_type=MESH)

    if pair == 2:
        greet((mate, x, y))
        greeted += 1
    for group, count in stages:
        me = member(sizes, group, here)
        for turn in range(1, count):
            greet(peer(sizes, group, here, (me + turn) % count))
            greeted += 1
    known = any(group == ("chip", "sx", "sy") for group, _ in stages)
    for dx, dy in ways:
        @pl.when(inside(dx, dy))
        def _():
            if pair == 2:
                greet((mate, x + dx, y + dy))
            if not known:
                greet((d, x + dx, y + dy))
    for dx, dy in ways:
        greeted = greeted + jnp.where(inside(dx, dy), pair - 1 + (0 if known else 1), 0)

    def edge(step, size):
        return pl.ds(1, size) if step == 0 else (1 if step == -1 else size)

    def rim(step, size):
        return pl.ds(1, size) if step == 0 else (0 if step == -1 else size + 1)

    def halo_copy(kind, slot, dx, dy):
        kinds = 0 if kind == 0 else pl.ds(1, 2)
        return pltpu.make_async_remote_copy(
            src_ref=planes.at[0, kinds, edge(dy, cells_y), edge(dx, cells_x)],
            dst_ref=planes.at[slot, kinds, rim(-dy, cells_y), rim(-dx, cells_x)],
            send_sem=halo_send.at[ways.index((dx, dy))],
            recv_sem=halo_recv.at[kind, ways.index((-dx, -dy))],
            device_id=(mate if slot else d, x + dx, y + dy),
            device_id_type=MESH,
        )

    def whole(ref, send_sem, recv_sem):
        return pltpu.make_async_remote_copy(
            src_ref=ref, dst_ref=ref, send_sem=send_sem, recv_sem=recv_sem,
            device_id=(mate, x, y), device_id_type=MESH,
        )

    def halo_arrived(kind):
        for n, (dx, dy) in enumerate(ways):
            @pl.when(inside(dx, dy))
            def _():
                where = (rim(dy, cells_y), rim(dx, cells_x))
                ref = planes.at[:, 0, *where] if kind == 0 else planes.at[0, pl.ds(1, 2), *where]
                whole(ref, halo_send.at[n], halo_recv.at[kind, n]).wait_recv()

    def halo_left():
        for n, (dx, dy) in enumerate(ways):
            @pl.when(inside(dx, dy))
            def _():
                where = (edge(dy, cells_y), edge(dx, cells_x))
                ref = planes.at[:, pl.ds(0, 2), *where] if pair == 2 else planes.at[0, :, *where]
                whole(ref, halo_send.at[n], halo_recv.at[0, n]).wait_send()

    def send_halo(kind):
        for dx, dy in ways:
            @pl.when(inside(dx, dy))
            def _():
                halo_copy(kind, 0, dx, dy).start()
                if kind == 0 and pair == 2:
                    halo_copy(kind, 1, dx, dy).start()

    inner = (pl.ds(1, cells_y), pl.ds(1, cells_x))

    def pair_copy(kind):
        kinds = pl.ds(0, 1) if kind == 0 else pl.ds(1, 2)
        return pltpu.make_async_remote_copy(
            src_ref=planes.at[0, kinds, *inner],
            dst_ref=planes.at[1, kinds, *inner],
            send_sem=pair_send.at[0],
            recv_sem=pair_recv.at[kind],
            device_id=(mate, x, y),
            device_id_type=MESH,
        )

    for dx, dy in ways:
        @pl.when(jnp.logical_not(inside(dx, dy)))
        def _():
            where = (rim(dy, cells_y), rim(dx, cells_x))
            for ref in [planes.at[0, n, *where] for n in range(3)] + [
                planes.at[slot, 0, *where] for slot in range(1, pair)
            ]:
                ref[...] = jnp.zeros(ref.shape, jnp.bfloat16)

    loads[0].wait()
    acts_wide[...] = acts_in[...].astype(jnp.float32).reshape(acts_wide.shape)
    for row in range(cells_y):
        planes[0, 0, 1 + row, pl.ds(1, cells_x)] = (
            acts_wide[pl.ds(row, plane, stride=cells_y), :]
            .astype(jnp.bfloat16)
            .reshape(cells_x, deep, LANES)
        )
    pl.semaphore_wait(barrier, greeted)
    send_halo(0)
    if pair == 2:
        pair_copy(0).start()
    loads[1].wait()
    loads[2].wait()
    loads[3].start()
    pre_wide[...] = pre_in[...].astype(jnp.float32).reshape(pre_wide.shape)
    pool_wide[...] = pool_in[...].astype(jnp.float32).reshape(pool_wide.shape) * 0.125
    for half in range(cells_y // 2):
        upper = pool_wide[pl.ds(half, plane // 2, stride=cells_y // 2), :]
        upper = jnp.broadcast_to(
            upper.reshape(cells_x // 2, 1, deep, LANES), (cells_x // 2, 2, deep, LANES)
        ).reshape(plane, LANES)
        for row in (2 * half, 2 * half + 1):
            for odd in (0, 1):
                before = pre_wide[pl.ds(odd * cells_y + row, plane, stride=2 * cells_y), :]
                gate = (upper * jnp.where(before > 0, 1.0, 0.3)).astype(jnp.bfloat16)
                planes[0, 1 + odd, 1 + row, pl.ds(1, cells_x)] = gate.reshape(cells_x, deep, LANES)
    if pair == 2:
        pair_copy(1).start()
    send_halo(1)

    def shift_z(slot, odd, rows, cols):
        wide = planes[slot, 1 + odd, rows, cols].astype(jnp.float32)
        axis = wide.ndim - 2
        depth_z = lax.broadcasted_iota(jnp.int32, wide.shape, axis)
        if odd:
            away = jnp.where(depth_z == 0, 0.0, pltpu.roll(wide, 1, axis))
        else:
            away = jnp.where(depth_z == deep - 1, 0.0, pltpu.roll(wide, deep - 1, axis))
        far[slot, odd, rows, cols] = away.astype(jnp.bfloat16)

    def turn_planes(slot, rows, a_all):
        for row in rows:
            for a in a_all:
                piece = planes[slot, 0, row, pl.ds(1 + a, cells_x)].reshape(plane, LANES)
                turned[slot, 1 + a, :, pl.ds(row * plane, plane)] = piece.T

    bias = jnp.zeros((ROWS, chan_out), jnp.float32)
    middle = range(1, 1 + cells_y)
    for slot in range(pair):
        if slot:
            for kind in (0, 1):
                pair_copy(kind).wait_recv()
        for odd in (0, 1):
            for row in middle:
                shift_z(slot, odd, row, pl.ds(1, cells_x))
                wide = planes[slot, 1 + odd, row, pl.ds(1, cells_x)].astype(jnp.float32)
                bias = bias + jnp.sum(wide.reshape(-1, ROWS, chan_out), axis=0)
        turn_planes(slot, middle, (0,))
    bias = jnp.sum(bias, axis=0, keepdims=True)
    top = lax.broadcasted_iota(jnp.int32, (ROWS, chan_out), 0) == 0
    acc[bias_unit] = jnp.where(top, jnp.broadcast_to(bias, (ROWS, chan_out)), 0.0)
    spare = acc.shape[0] - bias_unit - 1
    if spare:
        acc[pl.ds(bias_unit + 1, spare)] = jnp.zeros((spare, ROWS, chan_out), jnp.float32)

    halo_arrived(0)
    for slot in range(pair):
        turn_planes(slot, range(cells_y + 2), (-1, 1))
        turn_planes(slot, (0, cells_y + 1), (0,))

    def flat(ref, slot, odd):
        return ref[slot, odd, inner[0], inner[1]].reshape(cells, LANES)

    term = None
    for slot in range(pair):
        for odd in (0, 1):
            if odd:
                kinds = ((far, 0), (planes, 2), (planes, 1))
            else:
                kinds = ((planes, 2), (planes, 1), (far, 1))
            rhs = jnp.concatenate([flat(ref, slot, n) for ref, n in kinds], axis=1)
            rows = pl.ds(pl.multiple_of(odd * chan_in + core * share, share), share)
            lhs = jnp.concatenate(
                [
                    turned[slot, a, rows, pl.ds(b * plane, cells)]
                    for a in range(3)
                    for b in range(3)
                ],
                axis=0,
            )
            piece = jnp.dot(lhs, rhs, preferred_element_type=jnp.float32)
            term = piece if term is None else term + piece
    for n in range(offsets // 3):
        for c in range(3):
            acc[pl.ds((3 * n + c) * units, units)] = term[
                n * share : (n + 1) * share, c * chan_out : (c + 1) * chan_out
            ].reshape(units, ROWS, chan_out)

    starts = [0]

    def span_of(stage, index):
        return pl.ds(starts[stage] + index * chunks[stage], chunks[stage])

    def offset_of(stage):
        return sum((stages[s][1] - 1) * chunks[s] for s in range(stage))

    def arrivals(stage):
        return pl.ds(offset_of(stage), (stages[stage][1] - 1) * chunks[stage])

    def send_reduce(stage):
        group, count = stages[stage]
        chunk = chunks[stage]
        me = member(sizes, group, here)
        rows = pl.ds(starts[stage], count * chunk)
        leaving[rows] = encode(acc[rows])
        for move in moves_of(sizes, group, REDUCE_WAY):
            index = moved(digits(sizes, group), me, move)
            pltpu.make_async_remote_copy(
                src_ref=leaving.at[span_of(stage, index)],
                dst_ref=landing.at[pl.ds(offset_of(stage) + (move - 1) * chunk, chunk)],
                send_sem=red_send.at[stage],
                recv_sem=red_recv.at[stage],
                device_id=peer(sizes, group, here, index),
                device_id_type=MESH,
            ).start()

    def take_reduce(stage):
        group, count = stages[stage]
        chunk = chunks[stage]
        own = starts[stage] + member(sizes, group, here) * chunk
        ref = landing.at[arrivals(stage)]
        copies = whole(ref, red_send.at[stage], red_recv.at[stage])
        copies.wait_recv()
        value = acc[pl.ds(own, chunk)]
        for turn in range(count - 1):
            value = value + decode(landing[pl.ds(offset_of(stage) + turn * chunk, chunk)])
        copies.wait_send()
        acc[pl.ds(own, chunk)] = value
        starts.append(own)

    def make_taps():
        loads[3].wait()
        blank = jnp.zeros((chan_in, chan_out), jnp.bfloat16)
        for n in range(offsets // 3):
            three = [weights_ref[3 * n + c] for c in range(3)]
            taps[n, pl.ds(0, chan_in)] = jnp.concatenate([blank] + three, axis=1)
            taps[n, pl.ds(chan_in, chan_in)] = jnp.concatenate(three + [blank], axis=1)

    def input_gradient():
        make_taps()
        halo_arrived(1)
        for odd in (0, 1):
            for row in (0, cells_y + 1):
                shift_z(0, odd, row, pl.ds(0, cells_x + 2))
            for col in (0, cells_x + 1):
                shift_z(0, odd, pl.ds(1, cells_y), col)
        sums = None
        for a in (-1, 0, 1):
            for b in (-1, 0, 1):
                ys, xs = pl.ds(1 - b, cells_y), pl.ds(1 - a, cells_x)
                lhs = jnp.concatenate(
                    [
                        ref[0, n, ys, xs].reshape(cells, LANES)
                        for ref, n in ((far, 0), (planes, 2), (planes, 1), (far, 1))
                    ],
                    axis=1,
                )
                piece = lax.dot_general(
                    lhs,
                    taps[3 * (a + 1) + b + 1],
                    (((1,), (1,)), ((), ())),
                    preferred_element_type=jnp.float32,
                )
                sums = piece if sums is None else sums + piece
        for row in range(cells_y):
            acts_wide[pl.ds(row, plane, stride=cells_y), :] = sums[row * plane : (row + 1) * plane]
        grad_ref[...] = acts_wide[...].astype(jnp.bfloat16).reshape(grad_ref.shape)

    for stage in range(depth):
        send_reduce(stage)
        if stage == 0:
            input_gradient()
        take_reduce(stage)

    own, chunk = starts[-1], chunks[-1]
    value = acc[pl.ds(own, chunk)] * (1.0 / (samples * sizes[0]))
    coded = encode(value)
    rest = pltpu.roll(value - decode(coded), 1, 1)
    unit = own + lax.broadcasted_iota(jnp.int32, value.shape, 0)
    row = lax.broadcasted_iota(jnp.int32, value.shape, 1)
    is_rest = jnp.logical_and(unit == bias_unit, row == 1)
    total[core, pl.ds(own, chunk)] = encode(jnp.where(is_rest, rest, value))

    def parts_of(count):
        return -(-(count - 1) // PARTS)

    def unfold(side, rows):
        wide_ref[side, rows] = decode(total[side, rows])

    def forward(part, rows):
        ref = total.at[core, rows]
        pltpu.make_async_remote_copy(
            src_ref=ref, dst_ref=ref, send_sem=fwd_send.at[0], recv_sem=fwd_recv.at[part],
            device_id=(mate, x, y), device_id_type=MESH,
        ).start()

    for stage in reversed(range(depth)):
        group, count = stages[stage]
        me = member(sizes, group, here)
        size = parts_of(count)
        ref = total.at[core, span_of(stage, me)]
        order = moves_of(sizes, group, GATHER_WAY)
        for early in ((True, False) if FIRST else (None,)):
            for n, move in enumerate(order):
                index = moved(digits(sizes, group), me, move)
                copy = pltpu.make_async_remote_copy(
                    src_ref=ref, dst_ref=ref, send_sem=gat_send.at[stage],
                    recv_sem=gat_recv.at[stage * PARTS + n // size],
                    device_id=peer(sizes, group, here, index), device_id_type=MESH,
                )
                if early is None:
                    copy.start()
                else:
                    pl.when((index == 0) if early else (index != 0))(copy.start)
        last = stage == 0
        if last and pair == 2:
            forward(0, span_of(stage, me))
        if stage == depth - 1:
            unfold(core, span_of(stage, me))
        for part in (reversed(range(PARTS)) if BACK else range(PARTS)):
            turns = order[part * size : (part + 1) * size]
            if not turns:
                continue
            origins = [moved(digits(sizes, group), me, move, -1) for move in turns]
            ref = total.at[0, pl.ds(0, len(turns) * chunks[stage])]
            whole(ref, gat_send.at[stage], gat_recv.at[stage * PARTS + part]).wait_recv()
            if last and pair == 2:
                for origin in origins:
                    forward(1 + part, span_of(stage, origin))
            for origin in origins:
                unfold(core, span_of(stage, origin))
    group, count = stages[0]
    me = member(sizes, group, here)
    size = parts_of(count)
    if pair == 2:
        for part in ([0] + list(reversed(range(1, PARTS + 1))) if BACK else range(PARTS + 1)):
            turns = order[(part - 1) * size : part * size] if part else [0]
            if not turns:
                continue
            ref = total.at[0, pl.ds(0, len(turns) * chunks[0])]
            whole(ref, fwd_send.at[0], fwd_recv.at[part]).wait_recv()
            for move in turns:
                origin = moved(digits(sizes, group), me, move, -1)
                unfold(1 - core, span_of(0, origin))
    bias_ref[...] = wide_ref[0, bias_unit, pl.ds(0, 1)] + wide_ref[0, bias_unit, pl.ds(1, 1)]
    for stage in range(depth):
        ref = total.at[0, pl.ds(0, (stages[stage][1] - 1) * chunks[stage])]
        whole(ref, gat_send.at[stage], gat_recv.at[stage * PARTS]).wait_send()
    if pair == 2:
        whole(total.at[0], fwd_send.at[0], fwd_recv.at[0]).wait_send()
        ref = planes.at[0, :, *inner]
        whole(ref, pair_send.at[0], pair_recv.at[0]).wait_send()
    halo_left()


def fused(acts, before, upper, weights, cells_y, samples, sizes):
    cells_x, rows_acts, _ = acts.shape
    deep = rows_acts // cells_y
    offsets, chan_in, chan_out = weights.shape
    stages = plan_stages(sizes)
    pair = span("core", sizes)
    devices = 1
    for _, count in stages:
        devices *= count
    per_tap = chan_in // pair // ROWS
    step = math.lcm(devices, per_tap)
    units = -(-(offsets * per_tap + 1) // step) * step
    chunks = []
    for _, count in stages:
        chunks.append((chunks[-1] if chunks else units) // count)
    arriving = sum((count - 1) * chunk for (_, count), chunk in zip(stages, chunks))
    half, full = jnp.bfloat16, jnp.float32
    padded = (cells_y + 2, cells_x + 2, deep, LANES)
    cells = cells_x * rows_acts
    dma = pltpu.SemaphoreType.DMA
    scratch = [
        pltpu.VMEM(acts.shape, half),
        pltpu.VMEM(before.shape, half),
        pltpu.VMEM(upper.shape, half),
        pltpu.VMEM(weights.shape, half),
        pltpu.VMEM((cells, LANES), full),
        pltpu.VMEM((2 * cells, LANES), full),
        pltpu.VMEM((upper.shape[0] * upper.shape[1], LANES), full),
        pltpu.VMEM((pair, 3) + padded, half),
        pltpu.VMEM((pair, 2) + padded, half),
        pltpu.VMEM((pair, 3, LANES, (cells_y + 2) * cells_x * deep), half),
        pltpu.VMEM((offsets // 3, LANES, 4 * chan_out), half),
        pltpu.VMEM((units, ROWS, chan_out), full),
        pltpu.VMEM((pair, units, ROWS, chan_out), half),
        pltpu.VMEM((arriving, ROWS, chan_out), half),
        pltpu.VMEM((units, ROWS, chan_out), half),
        dma((4,)),
        dma((8,)),
        dma((2, 8)),
        dma((1,)),
        dma((2,)),
        dma((len(stages),)),
        dma((len(stages),)),
        dma((len(stages),)),
        dma((len(stages) * PARTS,)),
        dma((1,)),
        dma((PARTS + 1,)),
    ]
    return pl.pallas_call(
        functools.partial(body, sizes, stages, chunks, samples),
        out_shape=(
            pltpu.VMEM(acts.shape, half),
            pltpu.VMEM((pair, units, ROWS, chan_out), full),
            pltpu.VMEM((1, chan_out), full),
        ),
        in_specs=[pl.BlockSpec(memory_space=pltpu.MemorySpace.HBM)] * 4,
        out_specs=(pl.BlockSpec(memory_space=pltpu.VMEM),) * 3,
        scratch_shapes=scratch,
        compiler_params=pltpu.CompilerParams(
            collective_id=0, has_side_effects=True, vmem_limit_bytes=VMEM_LIMIT
        ),
    )(acts, before, upper, weights)


def store(grad_in, wide_in, bias_in, grad_out, wide_out, bias_out, sems):
    pair, _, share, _ = wide_in.shape
    copies = [
        pltpu.make_async_copy(
            wide_in.at[side, pl.ds(0, wide_out.shape[0])],
            wide_out.at[:, pl.ds(side * share, share)],
            sems.at[2 + side],
        )
        for side in range(pair)
    ]
    copies.append(pltpu.make_async_copy(grad_in, grad_out, sems.at[0]))
    copies.append(pltpu.make_async_copy(bias_in, bias_out, sems.at[1]))
    for copy in copies:
        copy.start()
    for copy in copies:
        copy.wait()


def finish(grad, wide, bias, offsets):
    pair, _, share, chan_out = wide.shape
    return pl.pallas_call(
        store,
        out_shape=(
            jax.ShapeDtypeStruct(grad.shape, grad.dtype),
            jax.ShapeDtypeStruct((offsets, pair * share, chan_out), wide.dtype),
            jax.ShapeDtypeStruct(bias.shape, bias.dtype),
        ),
        in_specs=[pl.BlockSpec(memory_space=pltpu.VMEM)] * 3,
        out_specs=(pl.BlockSpec(memory_space=pltpu.MemorySpace.HBM),) * 3,
        scratch_shapes=[pltpu.SemaphoreType.DMA((2 + pair,))],
        compiler_params=pltpu.CompilerParams(vmem_limit_bytes=STORE_LIMIT),
    )(grad, wide, bias)


def fold(array):
    rows, cols, flat = array.shape
    array = array.reshape(rows, cols, flat // LANES, LANES).transpose(0, 2, 1, 3)
    return array.reshape(rows, flat // LANES * cols, LANES)


def on_device(sizes, activations, preact, pooled_grad, weights):
    samples, cells_x, cells_y, _ = activations.shape
    offsets, chan_in, chan_out = weights.shape
    acts = fold(activations.reshape(activations.shape[1:]))
    before = fold(preact.reshape(preact.shape[1:]))
    upper = fold(pooled_grad.reshape(pooled_grad.shape[1:]))
    grad, total, bias = fused(acts, before, upper, weights, cells_y, samples, sizes)
    pair = span("core", sizes)
    total = total.reshape(pair, -1, chan_in // pair, chan_out)
    grad, total, bias = finish(grad, total, bias, offsets)
    grad = grad.reshape(cells_x, -1, cells_y, LANES).transpose(0, 2, 1, 3)
    return (
        grad.reshape(activations.shape),
        total,
        bias.reshape(chan_out),
    )


def solution(mesh):
    sizes = tuple(mesh.shape[axis] for axis in AXES)
    placed = (P("dp", "sx", "sy", None), P("dp", "sx", "sy", None), P("dp", "sx", "sy", None), P())
    return jax.shard_map(
        functools.partial(on_device, sizes),
        mesh=mesh,
        in_specs=placed,
        out_specs=(P("dp", "sx", "sy", None), P(), P()),
        check_vma=False,
    )
```

```python
import functools
import math

import jax
import jax.numpy as jnp
from jax import lax
from jax.experimental import pallas as pl
from jax.experimental.pallas import tpu as pltpu
from jax.sharding import PartitionSpec as P

MESH = pl.DeviceIdType.MESH
AXES = ("dp", "sx", "sy")
ROWS = 8
LANES = 128
FACTORS = ("core", "chip", "sx", "sy")
CODE = 2.0**36
ONE_SHOT = 16
PARTS = 5
GROUPS = 3
BACK = 1
FIRST = 1
REDUCE_WAY = -1
GATHER_WAY = -1
VMEM_LIMIT = 56 * 1024 * 1024
STORE_LIMIT = 8 * 1024 * 1024


def span(name, sizes):
    pair = 2 if sizes[0] % 2 == 0 else 1
    return {"core": pair, "chip": sizes[0] // pair, "sx": sizes[1], "sy": sizes[2]}[name]


def plan_stages(sizes):
    rest = span("chip", sizes) * sizes[1] * sizes[2]
    groups = [("chip", "sx", "sy")] if rest <= ONE_SHOT else [("chip",), ("sx",), ("sy",)]
    stages = []
    for group in groups:
        count = 1
        for name in group:
            count *= span(name, sizes)
        if count > 1:
            stages.append((group, count))
    return stages


def digits(sizes, group):
    found = []
    for name in group:
        left = span(name, sizes)
        while left % 2 == 0:
            found.append(2)
            left //= 2
        if left > 1:
            found.append(left)
    return found


def moved(radices, index, move, way=1):
    result, weight = 0, 1
    for radix in reversed(radices):
        result = result + (index % radix + way * (move % radix) + radix) % radix * weight
        index, move, weight = index // radix, move // radix, weight * radix
    return result


def moves_of(sizes, group, way):
    count = 1
    for name in group:
        count *= span(name, sizes)

    def steps(move):
        total = 0
        for name in reversed(group):
            size = span(name, sizes)
            total += move % size
            move //= size
        return way * total

    return sorted(range(1, count), key=steps)


def place():
    return tuple(lax.axis_index(axis) for axis in AXES)


def split(sizes, here):
    d, x, y = here
    pair = span("core", sizes)
    return {"core": d % pair, "chip": d // pair, "sx": x, "sy": y}


def member(sizes, group, here):
    values = split(sizes, here)
    index = 0
    for name in group:
        index = index * span(name, sizes) + values[name]
    return index


def peer(sizes, group, here, index):
    values = split(sizes, here)
    for name in reversed(group):
        values[name] = index % span(name, sizes)
        index = index // span(name, sizes)
    return (values["chip"] * span("core", sizes) + values["core"], values["sx"], values["sy"])


def encode(value):
    scaled = value * CODE
    return (scaled * jnp.abs(scaled)).astype(jnp.bfloat16)


def decode(coded):
    wide = coded.astype(jnp.float32)
    root = jnp.sqrt(jnp.abs(wide)) * (1.0 / CODE)
    return jnp.where(wide < 0, -root, root)


def body(sizes, stages, chunks, samples, acts_hbm, pre_hbm, pool_hbm, weights_hbm,
         grad_ref, wide_ref, bias_ref, *scratch):
    (acts_in, pre_in, pool_in, weights_ref, acts_wide, pre_wide, pool_wide, planes, far,
     row_out, row_in, col_out, col_in,
     turned, taps, acc, total, landing, leaving, load_sem, halo_send, halo_recv,
     pair_send, pair_recv, red_send, red_recv, gat_send, gat_recv, fwd_send, fwd_recv) = scratch
    loads = [
        pltpu.make_async_copy(src, dst, load_sem.at[n])
        for n, (src, dst) in enumerate(
            ((acts_hbm, acts_in), (pre_hbm, pre_in), (pool_hbm, pool_in), (weights_hbm, weights_ref))
        )
    ]
    for load in loads[:3]:
        load.start()
    here = place()
    d, x, y = here
    pair = span("core", sizes)
    core = d % pair
    mate = d + 1 - 2 * core if pair == 2 else d
    cells_x = acts_in.shape[0]
    cells_y, deep = planes.shape[2] - 2, planes.shape[4]
    offsets, chan_in, chan_out = weights_hbm.shape
    share = chan_in // pair
    plane = cells_x * deep
    cells = cells_y * plane
    units = share // ROWS
    bias_unit = offsets * units
    depth = len(stages)
    ways = [(0, -1), (0, 1), (-1, 0), (1, 0), (-1, -1), (-1, 1), (1, -1), (1, 1)]

    def inside(dx, dy):
        ok = None
        for coord, step, size in ((x, dx, sizes[1]), (y, dy, sizes[2])):
            if step == -1:
                term = coord > 0
            elif step == 1:
                term = coord < size - 1
            else:
                continue
            ok = term if ok is None else jnp.logical_and(ok, term)
        return ok

    barrier = pltpu.get_barrier_semaphore()
    greeted = 0

    def greet(target):
        pl.semaphore_signal(barrier, inc=1, device_id=target, device_id_type=MESH)

    if pair == 2:
        greet((mate, x, y))
        greeted += 1
    for group, count in stages:
        me = member(sizes, group, here)
        for turn in range(1, count):
            greet(peer(sizes, group, here, (me + turn) % count))
            greeted += 1
    known = any(group == ("chip", "sx", "sy") for group, _ in stages)
    for dx, dy in ways:
        @pl.when(inside(dx, dy))
        def _():
            if pair == 2:
                greet((mate, x + dx, y + dy))
            if not known:
                greet((d, x + dx, y + dy))
    for dx, dy in ways:
        greeted = greeted + jnp.where(inside(dx, dy), pair - 1 + (0 if known else 1), 0)

    def edge(step, size):
        return pl.ds(1, size) if step == 0 else (1 if step == -1 else size)

    def rim(step, size):
        return pl.ds(1, size) if step == 0 else (0 if step == -1 else size + 1)

    def packed(dx, dy):
        return pair == 2 and (dx == 0 or dy == 0)

    def swapped(value, to_side):
        low, high = pltpu.roll(value, share, 2), pltpu.roll(value, LANES - share, 2)
        return jnp.where(to_side == 0, low, high)

    def pack(edge_cells, out, side):
        wide = edge_cells.astype(jnp.float32)
        half = wide.shape[0] // 2
        lane = lax.broadcasted_iota(jnp.int32, (half, deep, LANES), 2)
        for slot in (0, 1):
            to_side = core if slot == 0 else 1 - core
            value = jnp.where(
                (lane // share) % 2 == to_side, wide[:half], swapped(wide[half:], to_side)
            )
            out[side, slot] = value.astype(jnp.bfloat16)

    def unpack(dx, dy):
        land = row_in if dx == 0 else col_in
        for slot in (0, 1):
            first = land[(dx + dy + 1) // 2, slot]
            second = swapped(first.astype(jnp.float32), 1 - core).astype(jnp.bfloat16)
            ref = planes.at[slot, 0, rim(dy, cells_y), rim(dx, cells_x)]
            ref[...] = jnp.concatenate([first, second], axis=0)

    def halo_copy(kind, slot, dx, dy):
        if kind == 0 and packed(dx, dy):
            out, land = (row_out, row_in) if dx == 0 else (col_out, col_in)
            side = (dx + dy + 1) // 2
            src, dst = out.at[side, slot], land.at[1 - side, slot]
        else:
            kinds = 0 if kind == 0 else pl.ds(1, 2)
            src = planes.at[0, kinds, edge(dy, cells_y), edge(dx, cells_x)]
            dst = planes.at[slot, kinds, rim(-dy, cells_y), rim(-dx, cells_x)]
        return pltpu.make_async_remote_copy(
            src_ref=src,
            dst_ref=dst,
            send_sem=halo_send.at[ways.index((dx, dy))],
            recv_sem=halo_recv.at[kind, ways.index((-dx, -dy))],
            device_id=(mate if slot else d, x + dx, y + dy),
            device_id_type=MESH,
        )

    def whole(ref, send_sem, recv_sem):
        return pltpu.make_async_remote_copy(
            src_ref=ref, dst_ref=ref, send_sem=send_sem, recv_sem=recv_sem,
            device_id=(mate, x, y), device_id_type=MESH,
        )

    def halo_arrived(kind):
        for n, (dx, dy) in enumerate(ways):
            @pl.when(inside(dx, dy))
            def _():
                where = (rim(dy, cells_y), rim(dx, cells_x))
                if kind:
                    ref = planes.at[0, pl.ds(1, 2), *where]
                elif packed(dx, dy):
                    ref = (row_in if dx == 0 else col_in).at[(dx + dy + 1) // 2]
                else:
                    ref = planes.at[:, 0, *where]
                whole(ref, halo_send.at[n], halo_recv.at[kind, n]).wait_recv()
                if kind == 0 and packed(dx, dy):
                    unpack(dx, dy)

    def halo_left():
        for n, (dx, dy) in enumerate(ways):
            @pl.when(inside(dx, dy))
            def _():
                where = (edge(dy, cells_y), edge(dx, cells_x))
                ref = planes.at[0, :, *where]
                if pair == 2 and not packed(dx, dy):
                    ref = planes.at[:, pl.ds(0, 2), *where]
                whole(ref, halo_send.at[n], halo_recv.at[0, n]).wait_send()

    def send_halo(kind):
        for dx, dy in ways:
            @pl.when(inside(dx, dy))
            def _():
                halo_copy(kind, 0, dx, dy).start()
                if kind == 0 and pair == 2:
                    halo_copy(kind, 1, dx, dy).start()

    inner = (pl.ds(1, cells_y), pl.ds(1, cells_x))

    def pair_copy(kind):
        kinds = pl.ds(0, 1) if kind == 0 else pl.ds(1, 2)
        return pltpu.make_async_remote_copy(
            src_ref=planes.at[0, kinds, *inner],
            dst_ref=planes.at[1, kinds, *inner],
            send_sem=pair_send.at[0],
            recv_sem=pair_recv.at[kind],
            device_id=(mate, x, y),
            device_id_type=MESH,
        )

    for dx, dy in ways:
        @pl.when(jnp.logical_not(inside(dx, dy)))
        def _():
            where = (rim(dy, cells_y), rim(dx, cells_x))
            for ref in [planes.at[0, n, *where] for n in range(3)] + [
                planes.at[slot, 0, *where] for slot in range(1, pair)
            ]:
                ref[...] = jnp.zeros(ref.shape, jnp.bfloat16)

    loads[0].wait()
    acts_wide[...] = acts_in[...].astype(jnp.float32).reshape(acts_wide.shape)
    for row in range(cells_y):
        planes[0, 0, 1 + row, pl.ds(1, cells_x)] = (
            acts_wide[pl.ds(row, plane, stride=cells_y), :]
            .astype(jnp.bfloat16)
            .reshape(cells_x, deep, LANES)
        )
    if pair == 2:
        for side in (0, 1):
            pack(planes[0, 0, 1 + side * (cells_y - 1), inner[1]], row_out, side)
            pack(planes[0, 0, inner[0], 1 + side * (cells_x - 1)], col_out, side)
    pl.semaphore_wait(barrier, greeted)
    send_halo(0)
    if pair == 2:
        pair_copy(0).start()
    loads[1].wait()
    loads[2].wait()
    loads[3].start()
    pre_wide[...] = pre_in[...].astype(jnp.float32).reshape(pre_wide.shape)
    pool_wide[...] = pool_in[...].astype(jnp.float32).reshape(pool_wide.shape) * 0.125
    for half in range(cells_y // 2):
        upper = pool_wide[pl.ds(half, plane // 2, stride=cells_y // 2), :]
        upper = jnp.broadcast_to(
            upper.reshape(cells_x // 2, 1, deep, LANES), (cells_x // 2, 2, deep, LANES)
        ).reshape(plane, LANES)
        for row in (2 * half, 2 * half + 1):
            for odd in (0, 1):
                before = pre_wide[pl.ds(odd * cells_y + row, plane, stride=2 * cells_y), :]
                gate = (upper * jnp.where(before > 0, 1.0, 0.3)).astype(jnp.bfloat16)
                planes[0, 1 + odd, 1 + row, pl.ds(1, cells_x)] = gate.reshape(cells_x, deep, LANES)
    if pair == 2:
        pair_copy(1).start()
    send_halo(1)

    def shift_z(slot, odd, rows, cols):
        wide = planes[slot, 1 + odd, rows, cols].astype(jnp.float32)
        axis = wide.ndim - 2
        depth_z = lax.broadcasted_iota(jnp.int32, wide.shape, axis)
        if odd:
            away = jnp.where(depth_z == 0, 0.0, pltpu.roll(wide, 1, axis))
        else:
            away = jnp.where(depth_z == deep - 1, 0.0, pltpu.roll(wide, deep - 1, axis))
        far[slot, odd, rows, cols] = away.astype(jnp.bfloat16)

    def turn_planes(slot, rows, a_all):
        for row in rows:
            for a in a_all:
                piece = planes[slot, 0, row, pl.ds(1 + a, cells_x)].reshape(plane, LANES)
                turned[slot, 1 + a, :, pl.ds(row * plane, plane)] = piece.T

    bias = jnp.zeros((ROWS, chan_out), jnp.float32)
    middle = range(1, 1 + cells_y)
    for slot in range(pair):
        if slot:
            for kind in (0, 1):
                pair_copy(kind).wait_recv()
        for odd in (0, 1):
            for row in middle:
                shift_z(slot, odd, row, pl.ds(1, cells_x))
                wide = planes[slot, 1 + odd, row, pl.ds(1, cells_x)].astype(jnp.float32)
                bias = bias + jnp.sum(wide.reshape(-1, ROWS, chan_out), axis=0)
        turn_planes(slot, middle, (0,))
    bias = jnp.sum(bias, axis=0, keepdims=True)
    top = lax.broadcasted_iota(jnp.int32, (ROWS, chan_out), 0) == 0
    acc[bias_unit] = jnp.where(top, jnp.broadcast_to(bias, (ROWS, chan_out)), 0.0)
    spare = acc.shape[0] - bias_unit - 1
    if spare:
        acc[pl.ds(bias_unit + 1, spare)] = jnp.zeros((spare, ROWS, chan_out), jnp.float32)

    halo_arrived(0)
    for slot in range(pair):
        turn_planes(slot, range(cells_y + 2), (-1, 1))
        turn_planes(slot, (0, cells_y + 1), (0,))

    def flat(ref, slot, odd):
        return ref[slot, odd, inner[0], inner[1]].reshape(cells, LANES)

    term = None
    for slot in range(pair):
        for odd in (0, 1):
            if odd:
                kinds = ((far, 0), (planes, 2), (planes, 1))
            else:
                kinds = ((planes, 2), (planes, 1), (far, 1))
            rhs = jnp.concatenate([flat(ref, slot, n) for ref, n in kinds], axis=1)
            rows = pl.ds(pl.multiple_of(odd * chan_in + core * share, share), share)
            lhs = jnp.concatenate(
                [
                    turned[slot, a, rows, pl.ds(b * plane, cells)]
                    for a in range(3)
                    for b in range(3)
                ],
                axis=0,
            )
            piece = jnp.dot(lhs, rhs, preferred_element_type=jnp.float32)
            term = piece if term is None else term + piece
    for n in range(offsets // 3):
        for c in range(3):
            acc[pl.ds((3 * n + c) * units, units)] = term[
                n * share : (n + 1) * share, c * chan_out : (c + 1) * chan_out
            ].reshape(units, ROWS, chan_out)

    starts = [0]

    def span_of(stage, index):
        return pl.ds(starts[stage] + index * chunks[stage], chunks[stage])

    def offset_of(stage):
        return sum((stages[s][1] - 1) * chunks[s] for s in range(stage))

    def arrivals(stage):
        return pl.ds(offset_of(stage), (stages[stage][1] - 1) * chunks[stage])

    def send_reduce(stage):
        group, count = stages[stage]
        chunk = chunks[stage]
        me = member(sizes, group, here)
        rows = pl.ds(starts[stage], count * chunk)
        leaving[rows] = encode(acc[rows])
        order = moves_of(sizes, group, REDUCE_WAY)
        size = -(-(count - 1) // GROUPS)
        for n, move in enumerate(order):
            index = moved(digits(sizes, group), me, move)
            pltpu.make_async_remote_copy(
                src_ref=leaving.at[span_of(stage, index)],
                dst_ref=landing.at[pl.ds(offset_of(stage) + (move - 1) * chunk, chunk)],
                send_sem=red_send.at[stage],
                recv_sem=red_recv.at[stage * GROUPS + n // size],
                device_id=peer(sizes, group, here, index),
                device_id_type=MESH,
            ).start()

    def take_reduce(stage):
        group, count = stages[stage]
        chunk = chunks[stage]
        own = starts[stage] + member(sizes, group, here) * chunk
        value = acc[pl.ds(own, chunk)]
        order = moves_of(sizes, group, REDUCE_WAY)
        size = -(-(count - 1) // GROUPS)
        for part in reversed(range(GROUPS)):
            turns = order[part * size : (part + 1) * size]
            if not turns:
                continue
            ref = landing.at[pl.ds(0, len(turns) * chunk)]
            whole(ref, red_send.at[stage], red_recv.at[stage * GROUPS + part]).wait_recv()
            for move in turns:
                value = value + decode(landing[pl.ds(offset_of(stage) + (move - 1) * chunk, chunk)])
        whole(landing.at[arrivals(stage)], red_send.at[stage], red_recv.at[stage]).wait_send()
        acc[pl.ds(own, chunk)] = value
        starts.append(own)

    def make_taps():
        loads[3].wait()
        blank = jnp.zeros((chan_in, chan_out), jnp.bfloat16)
        for n in range(offsets // 3):
            three = [weights_ref[3 * n + c] for c in range(3)]
            taps[n, pl.ds(0, chan_in)] = jnp.concatenate([blank] + three, axis=1)
            taps[n, pl.ds(chan_in, chan_in)] = jnp.concatenate(three + [blank], axis=1)

    def input_gradient():
        make_taps()
        halo_arrived(1)
        for odd in (0, 1):
            for row in (0, cells_y + 1):
                shift_z(0, odd, row, pl.ds(0, cells_x + 2))
            for col in (0, cells_x + 1):
                shift_z(0, odd, pl.ds(1, cells_y), col)
        sums = None
        for a in (-1, 0, 1):
            for b in (-1, 0, 1):
                ys, xs = pl.ds(1 - b, cells_y), pl.ds(1 - a, cells_x)
                lhs = jnp.concatenate(
                    [
                        ref[0, n, ys, xs].reshape(cells, LANES)
                        for ref, n in ((far, 0), (planes, 2), (planes, 1), (far, 1))
                    ],
                    axis=1,
                )
                piece = lax.dot_general(
                    lhs,
                    taps[3 * (a + 1) + b + 1],
                    (((1,), (1,)), ((), ())),
                    preferred_element_type=jnp.float32,
                )
                sums = piece if sums is None else sums + piece
        for row in range(cells_y):
            acts_wide[pl.ds(row, plane, stride=cells_y), :] = sums[row * plane : (row + 1) * plane]
        grad_ref[...] = acts_wide[...].astype(jnp.bfloat16).reshape(grad_ref.shape)

    for stage in range(depth):
        send_reduce(stage)
        if stage == 0:
            input_gradient()
        take_reduce(stage)

    own, chunk = starts[-1], chunks[-1]
    value = acc[pl.ds(own, chunk)] * (1.0 / (samples * sizes[0]))
    coded = encode(value)
    rest = pltpu.roll(value - decode(coded), 1, 1)
    unit = own + lax.broadcasted_iota(jnp.int32, value.shape, 0)
    row = lax.broadcasted_iota(jnp.int32, value.shape, 1)
    is_rest = jnp.logical_and(unit == bias_unit, row == 1)
    total[core, pl.ds(own, chunk)] = encode(jnp.where(is_rest, rest, value))

    def parts_of(count):
        return -(-(count - 1) // PARTS)

    def unfold(side, rows):
        wide_ref[side, rows] = decode(total[side, rows])

    def forward(part, rows):
        ref = total.at[core, rows]
        pltpu.make_async_remote_copy(
            src_ref=ref, dst_ref=ref, send_sem=fwd_send.at[0], recv_sem=fwd_recv.at[part],
            device_id=(mate, x, y), device_id_type=MESH,
        ).start()

    for stage in reversed(range(depth)):
        group, count = stages[stage]
        me = member(sizes, group, here)
        size = parts_of(count)
        ref = total.at[core, span_of(stage, me)]
        order = moves_of(sizes, group, GATHER_WAY)
        for early in ((True, False) if FIRST else (None,)):
            for n, move in enumerate(order):
                index = moved(digits(sizes, group), me, move)
                copy = pltpu.make_async_remote_copy(
                    src_ref=ref, dst_ref=ref, send_sem=gat_send.at[stage],
                    recv_sem=gat_recv.at[stage * PARTS + n // size],
                    device_id=peer(sizes, group, here, index), device_id_type=MESH,
                )
                if early is None:
                    copy.start()
                else:
                    pl.when((index == 0) if early else (index != 0))(copy.start)
        last = stage == 0
        if last and pair == 2:
            forward(0, span_of(stage, me))
        if stage == depth - 1:
            unfold(core, span_of(stage, me))
        for part in (reversed(range(PARTS)) if BACK else range(PARTS)):
            turns = order[part * size : (part + 1) * size]
            if not turns:
                continue
            origins = [moved(digits(sizes, group), me, move, -1) for move in turns]
            ref = total.at[0, pl.ds(0, len(turns) * chunks[stage])]
            whole(ref, gat_send.at[stage], gat_recv.at[stage * PARTS + part]).wait_recv()
            if last and pair == 2:
                for origin in origins:
                    forward(1 + part, span_of(stage, origin))
            for origin in origins:
                unfold(core, span_of(stage, origin))
    group, count = stages[0]
    me = member(sizes, group, here)
    size = parts_of(count)
    if pair == 2:
        for part in ([0] + list(reversed(range(1, PARTS + 1))) if BACK else range(PARTS + 1)):
            turns = order[(part - 1) * size : part * size] if part else [0]
            if not turns:
                continue
            ref = total.at[0, pl.ds(0, len(turns) * chunks[0])]
            whole(ref, fwd_send.at[0], fwd_recv.at[part]).wait_recv()
            for move in turns:
                origin = moved(digits(sizes, group), me, move, -1)
                unfold(1 - core, span_of(0, origin))
    bias_ref[...] = wide_ref[0, bias_unit, pl.ds(0, 1)] + wide_ref[0, bias_unit, pl.ds(1, 1)]
    for stage in range(depth):
        ref = total.at[0, pl.ds(0, (stages[stage][1] - 1) * chunks[stage])]
        whole(ref, gat_send.at[stage], gat_recv.at[stage * PARTS]).wait_send()
    if pair == 2:
        whole(total.at[0], fwd_send.at[0], fwd_recv.at[0]).wait_send()
        ref = planes.at[0, :, *inner]
        whole(ref, pair_send.at[0], pair_recv.at[0]).wait_send()
    halo_left()


def fused(acts, before, upper, weights, cells_y, samples, sizes):
    cells_x, rows_acts, _ = acts.shape
    deep = rows_acts // cells_y
    offsets, chan_in, chan_out = weights.shape
    stages = plan_stages(sizes)
    pair = span("core", sizes)
    devices = 1
    for _, count in stages:
        devices *= count
    per_tap = chan_in // pair // ROWS
    step = math.lcm(devices, per_tap)
    units = -(-(offsets * per_tap + 1) // step) * step
    chunks = []
    for _, count in stages:
        chunks.append((chunks[-1] if chunks else units) // count)
    arriving = sum((count - 1) * chunk for (_, count), chunk in zip(stages, chunks))
    half, full = jnp.bfloat16, jnp.float32
    padded = (cells_y + 2, cells_x + 2, deep, LANES)
    cells = cells_x * rows_acts
    dma = pltpu.SemaphoreType.DMA
    scratch = [
        pltpu.VMEM(acts.shape, half),
        pltpu.VMEM(before.shape, half),
        pltpu.VMEM(upper.shape, half),
        pltpu.VMEM(weights.shape, half),
        pltpu.VMEM((cells, LANES), full),
        pltpu.VMEM((2 * cells, LANES), full),
        pltpu.VMEM((upper.shape[0] * upper.shape[1], LANES), full),
        pltpu.VMEM((pair, 3) + padded, half),
        pltpu.VMEM((pair, 2) + padded, half),
        pltpu.VMEM((2, pair, cells_x // 2, deep, LANES), half),
        pltpu.VMEM((2, pair, cells_x // 2, deep, LANES), half),
        pltpu.VMEM((2, pair, cells_y // 2, deep, LANES), half),
        pltpu.VMEM((2, pair, cells_y // 2, deep, LANES), half),
        pltpu.VMEM((pair, 3, LANES, (cells_y + 2) * cells_x * deep), half),
        pltpu.VMEM((offsets // 3, LANES, 4 * chan_out), half),
        pltpu.VMEM((units, ROWS, chan_out), full),
        pltpu.VMEM((pair, units, ROWS, chan_out), half),
        pltpu.VMEM((arriving, ROWS, chan_out), half),
        pltpu.VMEM((units, ROWS, chan_out), half),
        dma((4,)),
        dma((8,)),
        dma((2, 8)),
        dma((1,)),
        dma((2,)),
        dma((len(stages),)),
        dma((len(stages) * GROUPS,)),
        dma((len(stages),)),
        dma((len(stages) * PARTS,)),
        dma((1,)),
        dma((PARTS + 1,)),
    ]
    return pl.pallas_call(
        functools.partial(body, sizes, stages, chunks, samples),
        out_shape=(
            pltpu.VMEM(acts.shape, half),
            pltpu.VMEM((pair, units, ROWS, chan_out), full),
            pltpu.VMEM((1, chan_out), full),
        ),
        in_specs=[pl.BlockSpec(memory_space=pltpu.MemorySpace.HBM)] * 4,
        out_specs=(pl.BlockSpec(memory_space=pltpu.VMEM),) * 3,
        scratch_shapes=scratch,
        compiler_params=pltpu.CompilerParams(
            collective_id=0, has_side_effects=True, vmem_limit_bytes=VMEM_LIMIT
        ),
    )(acts, before, upper, weights)


def store(grad_in, wide_in, bias_in, grad_out, wide_out, bias_out, sems):
    pair, _, share, _ = wide_in.shape
    copies = [
        pltpu.make_async_copy(
            wide_in.at[side, pl.ds(0, wide_out.shape[0])],
            wide_out.at[:, pl.ds(side * share, share)],
            sems.at[2 + side],
        )
        for side in range(pair)
    ]
    copies.append(pltpu.make_async_copy(grad_in, grad_out, sems.at[0]))
    copies.append(pltpu.make_async_copy(bias_in, bias_out, sems.at[1]))
    for copy in copies:
        copy.start()
    for copy in copies:
        copy.wait()


def finish(grad, wide, bias, offsets):
    pair, _, share, chan_out = wide.shape
    return pl.pallas_call(
        store,
        out_shape=(
            jax.ShapeDtypeStruct(grad.shape, grad.dtype),
            jax.ShapeDtypeStruct((offsets, pair * share, chan_out), wide.dtype),
            jax.ShapeDtypeStruct(bias.shape, bias.dtype),
        ),
        in_specs=[pl.BlockSpec(memory_space=pltpu.VMEM)] * 3,
        out_specs=(pl.BlockSpec(memory_space=pltpu.MemorySpace.HBM),) * 3,
        scratch_shapes=[pltpu.SemaphoreType.DMA((2 + pair,))],
        compiler_params=pltpu.CompilerParams(vmem_limit_bytes=STORE_LIMIT),
    )(grad, wide, bias)


def fold(array):
    rows, cols, flat = array.shape
    array = array.reshape(rows, cols, flat // LANES, LANES).transpose(0, 2, 1, 3)
    return array.reshape(rows, flat // LANES * cols, LANES)


def on_device(sizes, activations, preact, pooled_grad, weights):
    samples, cells_x, cells_y, _ = activations.shape
    offsets, chan_in, chan_out = weights.shape
    acts = fold(activations.reshape(activations.shape[1:]))
    before = fold(preact.reshape(preact.shape[1:]))
    upper = fold(pooled_grad.reshape(pooled_grad.shape[1:]))
    grad, total, bias = fused(acts, before, upper, weights, cells_y, samples, sizes)
    pair = span("core", sizes)
    total = total.reshape(pair, -1, chan_in // pair, chan_out)
    grad, total, bias = finish(grad, total, bias, offsets)
    grad = grad.reshape(cells_x, -1, cells_y, LANES).transpose(0, 2, 1, 3)
    return (
        grad.reshape(activations.shape),
        total,
        bias.reshape(chan_out),
    )


def solution(mesh):
    sizes = tuple(mesh.shape[axis] for axis in AXES)
    placed = (P("dp", "sx", "sy", None), P("dp", "sx", "sy", None), P("dp", "sx", "sy", None), P())
    return jax.shard_map(
        functools.partial(on_device, sizes),
        mesh=mesh,
        in_specs=placed,
        out_specs=(P("dp", "sx", "sy", None), P(), P()),
        check_vma=False,
    )
```

```python
import functools
import itertools
import math

import jax
import jax.numpy as jnp
from jax import lax
from jax.experimental import pallas as pl
from jax.experimental.pallas import tpu as pltpu
from jax.sharding import PartitionSpec as P

MESH = pl.DeviceIdType.MESH
AXES = ("dp", "sx", "sy")
ROWS = 8
LANES = 128
FACTORS = ("core", "chip", "sx", "sy")
CODE = 2.0**36
ONE_SHOT = 16
PARTS = 4
NEAR = 2
VMEM_LIMIT = 56 * 1024 * 1024
STORE_LIMIT = 8 * 1024 * 1024


def span(name, sizes):
    pair = 2 if sizes[0] % 2 == 0 else 1
    return {"core": pair, "chip": sizes[0] // pair, "sx": sizes[1], "sy": sizes[2]}[name]


def plan_stages(sizes):
    rest = span("chip", sizes) * sizes[1] * sizes[2]
    groups = [("chip", "sx", "sy")] if rest <= ONE_SHOT else [("chip",), ("sx",), ("sy",)]
    stages = []
    for group in groups:
        count = 1
        for name in group:
            count *= span(name, sizes)
        if count > 1:
            stages.append((group, count))
    return stages


def digits(sizes, group):
    found = []
    for name in group:
        left = span(name, sizes)
        while left % 2 == 0:
            found.append(2)
            left //= 2
        if left > 1:
            found.append(left)
    return found


def moved(radices, index, move, way=1):
    result, weight = 0, 1
    for radix in reversed(radices):
        result = result + (index % radix + way * (move % radix) + radix) % radix * weight
        index, move, weight = index // radix, move // radix, weight * radix
    return result


def reach(sizes, group, here):
    values = split(sizes, here)
    ahead, behind = {}, {}
    for name in group:
        radices = digits(sizes, (name,))
        many = range(span(name, sizes))
        ahead[name] = [moved(radices, values[name], move) for move in many]
        behind[name] = ahead[name]
        if any(radix > 2 for radix in radices):
            behind[name] = [moved(radices, values[name], move, -1) for move in many]
    weights, weight = {}, 1
    for name in reversed(group):
        weights[name] = weight
        weight *= span(name, sizes)
    to, origin, device = [], [], []
    terms = {name: [value * weights[name] for value in ahead[name]] for name in group}
    terms_back = terms
    if any(behind[name] is not ahead[name] for name in group):
        terms_back = {name: [value * weights[name] for value in behind[name]] for name in group}
    pair = span("core", sizes)
    chips = [chip * pair + values["core"] for chip in ahead.get("chip", [values["chip"]])]
    for move in range(weight):
        at = {}
        for name in reversed(group):
            at[name] = move // weights[name] % span(name, sizes)
        to.append(sum(terms[name][at[name]] for name in group))
        origin.append(sum(terms_back[name][at[name]] for name in group))
        device.append(
            (
                chips[at.get("chip", 0)],
                ahead["sx"][at["sx"]] if "sx" in at else values["sx"],
                ahead["sy"][at["sy"]] if "sy" in at else values["sy"],
            )
        )
    return to, origin, device


def moves_of(sizes, group, way):
    count = 1
    for name in group:
        count *= span(name, sizes)

    def steps(move):
        total = 0
        for name in reversed(group):
            size = span(name, sizes)
            total += move % size
            move //= size
        return way * total

    return sorted(range(1, count), key=steps)


def place():
    return tuple(lax.axis_index(axis) for axis in AXES)


def split(sizes, here):
    d, x, y = here
    pair = span("core", sizes)
    return {"core": d % pair, "chip": d // pair, "sx": x, "sy": y}


def encode(value):
    scaled = value * CODE
    return (scaled * jnp.abs(scaled)).astype(jnp.bfloat16)


def decode(coded):
    wide = coded.astype(jnp.float32)
    root = jnp.sqrt(jnp.abs(wide)) * (1.0 / CODE)
    return jnp.where(wide < 0, -root, root)


def body(sizes, stages, chunks, samples, acts_hbm, pre_hbm, pool_hbm, weights_hbm,
         grad_ref, wide_ref, bias_ref, *scratch):
    (acts_in, pre_in, pool_in, weights_ref, acts_wide, pre_wide, pool_wide, planes, far,
     row_out, row_in, col_out, col_in,
     turned, taps, acc, total, landing, leaving, load_sem, halo_send, halo_recv,
     pair_send, pair_recv, red_send, red_recv, gat_send, gat_recv, fwd_send, fwd_recv) = scratch
    loads = [
        pltpu.make_async_copy(src, dst, load_sem.at[n])
        for n, (src, dst) in enumerate(
            ((acts_hbm, acts_in), (pre_hbm, pre_in), (pool_hbm, pool_in), (weights_hbm, weights_ref))
        )
    ]
    for load in loads[:3]:
        load.start()
    here = place()
    d, x, y = here
    pair = span("core", sizes)
    core = d % pair
    mate = d + 1 - 2 * core if pair == 2 else d
    cells_x = acts_in.shape[0]
    cells_y, deep = planes.shape[2] - 2, planes.shape[4]
    offsets, chan_in, chan_out = weights_hbm.shape
    share = chan_in // pair
    plane = cells_x * deep
    cells = cells_y * plane
    units = share // ROWS
    bias_unit = offsets * units
    depth = len(stages)
    routes = [reach(sizes, group, here) for group, _ in stages]
    ways = [(0, -1), (0, 1), (-1, 0), (1, 0), (-1, -1), (-1, 1), (1, -1), (1, 1)]

    def inside(dx, dy):
        ok = None
        for coord, step, size in ((x, dx, sizes[1]), (y, dy, sizes[2])):
            if step == -1:
                term = coord > 0
            elif step == 1:
                term = coord < size - 1
            else:
                continue
            ok = term if ok is None else jnp.logical_and(ok, term)
        return ok

    barrier = pltpu.get_barrier_semaphore()
    greeted = 0

    def greet(target):
        pl.semaphore_signal(barrier, inc=1, device_id=target, device_id_type=MESH)

    if pair == 2:
        greet((mate, x, y))
        greeted += 1
    for (group, _), (_, _, device) in zip(stages, routes):
        for move in moves_of(sizes, group, -1):
            greet(device[move])
            greeted += 1
    known = any(group == ("chip", "sx", "sy") for group, _ in stages)
    for dx, dy in ways:
        @pl.when(inside(dx, dy))
        def _():
            if pair == 2:
                greet((mate, x + dx, y + dy))
            if not known:
                greet((d, x + dx, y + dy))
    for dx, dy in ways:
        greeted = greeted + jnp.where(inside(dx, dy), pair - 1 + (0 if known else 1), 0)

    def edge(step, size):
        return pl.ds(1, size) if step == 0 else (1 if step == -1 else size)

    def rim(step, size):
        return pl.ds(1, size) if step == 0 else (0 if step == -1 else size + 1)

    def lane_of(dx, dy):
        near_x, near_y = (abs(dx) if sizes[1] <= 2 else dx), (abs(dy) if sizes[2] <= 2 else dy)
        return ways.index((near_x, near_y)) if (near_x or near_y) else 0

    used = sorted({lane_of(dx, dy) for dx, dy in ways})

    def packed(dx, dy):
        return pair == 2 and (dx == 0 or dy == 0)

    def swapped(value, to_side):
        low, high = pltpu.roll(value, share, 2), pltpu.roll(value, LANES - share, 2)
        return jnp.where(to_side == 0, low, high)

    def pack(edge_cells, out, side):
        wide = edge_cells.astype(jnp.float32)
        half = wide.shape[0] // 2
        lane = lax.broadcasted_iota(jnp.int32, (half, deep, LANES), 2)
        for slot in (0, 1):
            to_side = core if slot == 0 else 1 - core
            value = jnp.where(
                (lane // share) % 2 == to_side, wide[:half], swapped(wide[half:], to_side)
            )
            out[side, slot] = value.astype(jnp.bfloat16)

    def unpack(dx, dy):
        land = row_in if dx == 0 else col_in
        for slot in (0, 1):
            first = land[(dx + dy + 1) // 2, slot]
            second = swapped(first.astype(jnp.float32), 1 - core).astype(jnp.bfloat16)
            ref = planes.at[slot, 0, rim(dy, cells_y), rim(dx, cells_x)]
            ref[...] = jnp.concatenate([first, second], axis=0)

    def halo_copy(kind, slot, dx, dy):
        if kind == 0 and packed(dx, dy):
            out, land = (row_out, row_in) if dx == 0 else (col_out, col_in)
            side = (dx + dy + 1) // 2
            src, dst = out.at[side, slot], land.at[1 - side, slot]
        else:
            kinds = 0 if kind == 0 else pl.ds(1, 2)
            src = planes.at[0, kinds, edge(dy, cells_y), edge(dx, cells_x)]
            dst = planes.at[slot, kinds, rim(-dy, cells_y), rim(-dx, cells_x)]
        return pltpu.make_async_remote_copy(
            src_ref=src,
            dst_ref=dst,
            send_sem=halo_send.at[used.index(lane_of(dx, dy))],
            recv_sem=halo_recv.at[kind, used.index(lane_of(-dx, -dy))],
            device_id=(mate if slot else d, x + dx, y + dy),
            device_id_type=MESH,
        )

    def whole(ref, send_sem, recv_sem):
        return pltpu.make_async_remote_copy(
            src_ref=ref, dst_ref=ref, send_sem=send_sem, recv_sem=recv_sem,
            device_id=(mate, x, y), device_id_type=MESH,
        )

    def halo_arrived(kind):
        for dx, dy in ways:
            @pl.when(inside(dx, dy))
            def _():
                where = (rim(dy, cells_y), rim(dx, cells_x))
                if kind:
                    ref = planes.at[0, pl.ds(1, 2), *where]
                elif packed(dx, dy):
                    ref = (row_in if dx == 0 else col_in).at[(dx + dy + 1) // 2]
                else:
                    ref = planes.at[:, 0, *where]
                n = used.index(lane_of(dx, dy))
                whole(ref, halo_send.at[n], halo_recv.at[kind, n]).wait_recv()
                if kind == 0 and packed(dx, dy):
                    unpack(dx, dy)

    def halo_left():
        for dx, dy in ways:
            @pl.when(inside(dx, dy))
            def _():
                where = (edge(dy, cells_y), edge(dx, cells_x))
                ref = planes.at[0, :, *where]
                if pair == 2 and not packed(dx, dy):
                    ref = planes.at[:, pl.ds(0, 2), *where]
                n = used.index(lane_of(dx, dy))
                whole(ref, halo_send.at[n], halo_recv.at[0, n]).wait_send()

    def send_halo(kind):
        for dx, dy in ways:
            @pl.when(inside(dx, dy))
            def _():
                halo_copy(kind, 0, dx, dy).start()
                if kind == 0 and pair == 2:
                    halo_copy(kind, 1, dx, dy).start()

    inner = (pl.ds(1, cells_y), pl.ds(1, cells_x))

    def pair_copy(kind):
        kinds = pl.ds(0, 1) if kind == 0 else pl.ds(1, 2)
        return pltpu.make_async_remote_copy(
            src_ref=planes.at[0, kinds, *inner],
            dst_ref=planes.at[1, kinds, *inner],
            send_sem=pair_send.at[0],
            recv_sem=pair_recv.at[kind],
            device_id=(mate, x, y),
            device_id_type=MESH,
        )

    for dx, dy in ways:
        @pl.when(jnp.logical_not(inside(dx, dy)))
        def _():
            where = (rim(dy, cells_y), rim(dx, cells_x))
            for ref in [planes.at[0, n, *where] for n in range(3)] + [
                planes.at[slot, 0, *where] for slot in range(1, pair)
            ]:
                ref[...] = jnp.zeros(ref.shape, jnp.bfloat16)

    loads[0].wait()
    acts_wide[...] = acts_in[...].astype(jnp.float32).reshape(acts_wide.shape)
    for row in range(cells_y):
        planes[0, 0, 1 + row, pl.ds(1, cells_x)] = (
            acts_wide[pl.ds(row, plane, stride=cells_y), :]
            .astype(jnp.bfloat16)
            .reshape(cells_x, deep, LANES)
        )
    if pair == 2:
        for side in (0, 1):
            pack(planes[0, 0, 1 + side * (cells_y - 1), inner[1]], row_out, side)
            pack(planes[0, 0, inner[0], 1 + side * (cells_x - 1)], col_out, side)
    pl.semaphore_wait(barrier, greeted)
    send_halo(0)
    if pair == 2:
        pair_copy(0).start()
    loads[1].wait()
    loads[2].wait()
    loads[3].start()
    pre_wide[...] = pre_in[...].astype(jnp.float32).reshape(pre_wide.shape)
    pool_wide[...] = pool_in[...].astype(jnp.float32).reshape(pool_wide.shape) * 0.125
    for half in range(cells_y // 2):
        upper = pool_wide[pl.ds(half, plane // 2, stride=cells_y // 2), :]
        upper = jnp.broadcast_to(
            upper.reshape(cells_x // 2, 1, deep, LANES), (cells_x // 2, 2, deep, LANES)
        ).reshape(plane, LANES)
        for row in (2 * half, 2 * half + 1):
            for odd in (0, 1):
                before = pre_wide[pl.ds(odd * cells_y + row, plane, stride=2 * cells_y), :]
                gate = (upper * jnp.where(before > 0, 1.0, 0.3)).astype(jnp.bfloat16)
                planes[0, 1 + odd, 1 + row, pl.ds(1, cells_x)] = gate.reshape(cells_x, deep, LANES)
    if pair == 2:
        pair_copy(1).start()
    send_halo(1)

    def shift_z(slot, odd, rows, cols):
        wide = planes[slot, 1 + odd, rows, cols].astype(jnp.float32)
        axis = wide.ndim - 2
        depth_z = lax.broadcasted_iota(jnp.int32, wide.shape, axis)
        if odd:
            away = jnp.where(depth_z == 0, 0.0, pltpu.roll(wide, 1, axis))
        else:
            away = jnp.where(depth_z == deep - 1, 0.0, pltpu.roll(wide, deep - 1, axis))
        far[slot, odd, rows, cols] = away.astype(jnp.bfloat16)

    def turn_planes(slot, rows, a_all):
        for row in rows:
            for a in a_all:
                piece = planes[slot, 0, row, pl.ds(1 + a, cells_x)].reshape(plane, LANES)
                turned[slot, 1 + a, :, pl.ds(row * plane, plane)] = piece.T

    bias = jnp.zeros((ROWS, chan_out), jnp.float32)
    middle = range(1, 1 + cells_y)
    for slot in range(pair):
        if slot:
            for kind in (0, 1):
                pair_copy(kind).wait_recv()
        for odd in (0, 1):
            for row in middle:
                shift_z(slot, odd, row, pl.ds(1, cells_x))
                wide = planes[slot, 1 + odd, row, pl.ds(1, cells_x)].astype(jnp.float32)
                bias = bias + jnp.sum(wide.reshape(-1, ROWS, chan_out), axis=0)
        turn_planes(slot, middle, (0,))
    bias = jnp.sum(bias, axis=0, keepdims=True)
    top = lax.broadcasted_iota(jnp.int32, (ROWS, chan_out), 0) == 0
    acc[bias_unit] = jnp.where(top, jnp.broadcast_to(bias, (ROWS, chan_out)), 0.0)
    spare = acc.shape[0] - bias_unit - 1
    if spare:
        acc[pl.ds(bias_unit + 1, spare)] = jnp.zeros((spare, ROWS, chan_out), jnp.float32)

    halo_arrived(0)
    for slot in range(pair):
        turn_planes(slot, range(cells_y + 2), (-1, 1))
        turn_planes(slot, (0, cells_y + 1), (0,))

    def flat(ref, slot, odd):
        return ref[slot, odd, inner[0], inner[1]].reshape(cells, LANES)

    term = None
    for slot in range(pair):
        for odd in (0, 1):
            if odd:
                kinds = ((far, 0), (planes, 2), (planes, 1))
            else:
                kinds = ((planes, 2), (planes, 1), (far, 1))
            rhs = jnp.concatenate([flat(ref, slot, n) for ref, n in kinds], axis=1)
            rows = pl.ds(pl.multiple_of(odd * chan_in + core * share, share), share)
            lhs = jnp.concatenate(
                [
                    turned[slot, a, rows, pl.ds(b * plane, cells)]
                    for a in range(3)
                    for b in range(3)
                ],
                axis=0,
            )
            piece = jnp.dot(lhs, rhs, preferred_element_type=jnp.float32)
            term = piece if term is None else term + piece
    for n in range(offsets // 3):
        for c in range(3):
            acc[pl.ds((3 * n + c) * units, units)] = term[
                n * share : (n + 1) * share, c * chan_out : (c + 1) * chan_out
            ].reshape(units, ROWS, chan_out)

    starts = [0]

    def span_of(stage, index):
        return pl.ds(starts[stage] + index * chunks[stage], chunks[stage])

    def offset_of(stage):
        return sum((stages[s][1] - 1) * chunks[s] for s in range(stage))

    def arrivals(stage):
        return pl.ds(offset_of(stage), (stages[stage][1] - 1) * chunks[stage])

    def at_last(target, name, last):
        if name == "chip":
            return (last * pair + core,) + target[1:]
        return target[:1] + ((last, target[2]) if name == "sx" else (target[1], last))

    def send_reduce(stage):
        group, count = stages[stage]
        chunk = chunks[stage]
        to, _, device = routes[stage]
        rows = pl.ds(starts[stage], count * chunk)
        leaving[rows] = encode(acc[rows])
        name = group[-1]
        deep_last = span(name, sizes)
        own_last = split(sizes, here)[name]
        for last in reversed(range(deep_last)):
            step = (last - own_last + deep_last) % deep_last
            for first in reversed(range(0, count, deep_last)):
                index = to[first] - own_last + last
                copy = pltpu.make_async_remote_copy(
                    src_ref=leaving.at[span_of(stage, index)],
                    dst_ref=landing.at[pl.ds(offset_of(stage) + (first + step - 1) * chunk, chunk)],
                    send_sem=red_send.at[stage],
                    recv_sem=red_recv.at[stage],
                    device_id=at_last(device[first], name, last),
                    device_id_type=MESH,
                )
                if first:
                    copy.start()
                else:
                    pl.when(own_last != last)(copy.start)

    def take_reduce(stage):
        group, count = stages[stage]
        chunk = chunks[stage]
        own = starts[stage] + routes[stage][0][0] * chunk
        value = acc[pl.ds(own, chunk)]
        copies = whole(landing.at[arrivals(stage)], red_send.at[stage], red_recv.at[stage])
        copies.wait_recv()
        for turn in range(count - 1):
            value = value + decode(landing[pl.ds(offset_of(stage) + turn * chunk, chunk)])
        copies.wait_send()
        acc[pl.ds(own, chunk)] = value
        starts.append(own)

    def make_taps():
        loads[3].wait()
        blank = jnp.zeros((chan_in, chan_out), jnp.bfloat16)
        for n in range(offsets // 3):
            three = [weights_ref[3 * n + c] for c in range(3)]
            taps[n, pl.ds(0, chan_in)] = jnp.concatenate([blank] + three, axis=1)
            taps[n, pl.ds(chan_in, chan_in)] = jnp.concatenate(three + [blank], axis=1)

    def input_gradient():
        make_taps()
        halo_arrived(1)
        for odd in (0, 1):
            for row in (0, cells_y + 1):
                shift_z(0, odd, row, pl.ds(0, cells_x + 2))
            for col in (0, cells_x + 1):
                shift_z(0, odd, pl.ds(1, cells_y), col)
        sums = None
        for a in (-1, 0, 1):
            for b in (-1, 0, 1):
                ys, xs = pl.ds(1 - b, cells_y), pl.ds(1 - a, cells_x)
                lhs = jnp.concatenate(
                    [
                        ref[0, n, ys, xs].reshape(cells, LANES)
                        for ref, n in ((far, 0), (planes, 2), (planes, 1), (far, 1))
                    ],
                    axis=1,
                )
                piece = lax.dot_general(
                    lhs,
                    taps[3 * (a + 1) + b + 1],
                    (((1,), (1,)), ((), ())),
                    preferred_element_type=jnp.float32,
                )
                sums = piece if sums is None else sums + piece
        for row in range(cells_y):
            acts_wide[pl.ds(row, plane, stride=cells_y), :] = sums[row * plane : (row + 1) * plane]
        grad_ref[...] = acts_wide[...].astype(jnp.bfloat16).reshape(grad_ref.shape)

    for stage in range(depth):
        send_reduce(stage)
        if stage == 0:
            input_gradient()
        take_reduce(stage)

    own, chunk = starts[-1], chunks[-1]
    value = acc[pl.ds(own, chunk)] * (1.0 / (samples * sizes[0]))
    coded = encode(value)
    rest = pltpu.roll(value - decode(coded), 1, 1)
    unit = own + lax.broadcasted_iota(jnp.int32, value.shape, 0)
    row = lax.broadcasted_iota(jnp.int32, value.shape, 1)
    is_rest = jnp.logical_and(unit == bias_unit, row == 1)
    total[core, pl.ds(own, chunk)] = encode(jnp.where(is_rest, rest, value))

    def unfold(side, rows):
        wide_ref[side, rows] = decode(total[side, rows])

    def forward(part, rows):
        ref = total.at[core, rows]
        pltpu.make_async_remote_copy(
            src_ref=ref, dst_ref=ref, send_sem=fwd_send.at[0], recv_sem=fwd_recv.at[part],
            device_id=(mate, x, y), device_id_type=MESH,
        ).start()

    for stage in reversed(range(depth)):
        group, count = stages[stage]
        to, origin, device = routes[stage]
        me = to[0]
        ref = total.at[core, span_of(stage, me)]
        name = group[-1]
        deep_last = span(name, sizes)
        own_last = split(sizes, here)[name]
        firsts = list(reversed(range(0, count, deep_last)))
        nearby = {first: 0 for first in firsts}
        if len(group) > 1:
            nearby = {first: device[first][0] // pair + device[first][1] for first in firsts}
        for rank, first, last in itertools.product(range(NEAR + 1), firsts, range(deep_last)):
            if last > rank and rank < NEAR:
                continue
            copy = pltpu.make_async_remote_copy(
                src_ref=ref, dst_ref=ref, send_sem=gat_send.at[stage],
                recv_sem=gat_recv.at[stage * PARTS + first // deep_last],
                device_id=at_last(device[first], name, last), device_id_type=MESH,
            )
            steps = nearby[first] + last
            ok = (steps == rank) if rank < NEAR else (steps >= rank)
            if not first:
                ok = jnp.logical_and(ok, own_last != last)
            pl.when(ok)(copy.start)

        def sources(first):
            return [
                origin[first] - own_last + (own_last + turn) % deep_last
                for turn in range(0 if first else 1, deep_last)
            ]

        last = stage == 0
        if last and pair == 2:
            forward(0, span_of(stage, me))
        if stage == depth - 1:
            unfold(core, span_of(stage, me))
        for first in reversed(firsts):
            part = first // deep_last
            origins = sources(first)
            if not origins:
                continue
            ref = total.at[0, pl.ds(0, len(origins) * chunks[stage])]
            whole(ref, gat_send.at[stage], gat_recv.at[stage * PARTS + part]).wait_recv()
            if last and pair == 2:
                for index in origins:
                    forward(1 + part, span_of(stage, index))
            for index in origins:
                unfold(core, span_of(stage, index))
    if pair == 2:
        for part in range(len(firsts) + 1):
            origins = sources((part - 1) * deep_last) if part else [me]
            if not origins:
                continue
            ref = total.at[0, pl.ds(0, len(origins) * chunks[0])]
            whole(ref, fwd_send.at[0], fwd_recv.at[part]).wait_recv()
            for index in origins:
                unfold(1 - core, span_of(0, index))
    bias_ref[...] = wide_ref[0, bias_unit, pl.ds(0, 1)] + wide_ref[0, bias_unit, pl.ds(1, 1)]
    for stage in range(depth):
        ref = total.at[0, pl.ds(0, (stages[stage][1] - 1) * chunks[stage])]
        whole(ref, gat_send.at[stage], gat_recv.at[stage * PARTS]).wait_send()
    if pair == 2:
        whole(total.at[0], fwd_send.at[0], fwd_recv.at[0]).wait_send()
        ref = planes.at[0, :, *inner]
        whole(ref, pair_send.at[0], pair_recv.at[0]).wait_send()
    halo_left()


def fused(acts, before, upper, weights, cells_y, samples, sizes):
    cells_x, rows_acts, _ = acts.shape
    deep = rows_acts // cells_y
    offsets, chan_in, chan_out = weights.shape
    stages = plan_stages(sizes)
    pair = span("core", sizes)
    devices = 1
    for _, count in stages:
        devices *= count
    per_tap = chan_in // pair // ROWS
    step = math.lcm(devices, per_tap)
    units = -(-(offsets * per_tap + 1) // step) * step
    chunks = []
    for _, count in stages:
        chunks.append((chunks[-1] if chunks else units) // count)
    arriving = sum((count - 1) * chunk for (_, count), chunk in zip(stages, chunks))
    half, full = jnp.bfloat16, jnp.float32
    padded = (cells_y + 2, cells_x + 2, deep, LANES)
    cells = cells_x * rows_acts
    dma = pltpu.SemaphoreType.DMA
    lanes = (2 if sizes[1] <= 2 else 3) * (2 if sizes[2] <= 2 else 3) - 1
    scratch = [
        pltpu.VMEM(acts.shape, half),
        pltpu.VMEM(before.shape, half),
        pltpu.VMEM(upper.shape, half),
        pltpu.VMEM(weights.shape, half),
        pltpu.VMEM((cells, LANES), full),
        pltpu.VMEM((2 * cells, LANES), full),
        pltpu.VMEM((upper.shape[0] * upper.shape[1], LANES), full),
        pltpu.VMEM((pair, 3) + padded, half),
        pltpu.VMEM((pair, 2) + padded, half),
        pltpu.VMEM((2, pair, cells_x // 2, deep, LANES), half),
        pltpu.VMEM((2, pair, cells_x // 2, deep, LANES), half),
        pltpu.VMEM((2, pair, cells_y // 2, deep, LANES), half),
        pltpu.VMEM((2, pair, cells_y // 2, deep, LANES), half),
        pltpu.VMEM((pair, 3, LANES, (cells_y + 2) * cells_x * deep), half),
        pltpu.VMEM((offsets // 3, LANES, 4 * chan_out), half),
        pltpu.VMEM((units, ROWS, chan_out), full),
        pltpu.VMEM((pair, units, ROWS, chan_out), half),
        pltpu.VMEM((arriving, ROWS, chan_out), half),
        pltpu.VMEM((units, ROWS, chan_out), half),
        dma((4,)),
        dma((lanes,)),
        dma((2, lanes)),
        dma((1,)),
        dma((2,)),
        dma((len(stages),)),
        dma((len(stages),)),
        dma((len(stages),)),
        dma((len(stages) * PARTS,)),
        dma((1,)),
        dma((PARTS + 1,)),
    ]
    return pl.pallas_call(
        functools.partial(body, sizes, stages, chunks, samples),
        out_shape=(
            pltpu.VMEM(acts.shape, half),
            pltpu.VMEM((pair, units, ROWS, chan_out), full),
            pltpu.VMEM((1, chan_out), full),
        ),
        in_specs=[pl.BlockSpec(memory_space=pltpu.MemorySpace.HBM)] * 4,
        out_specs=(pl.BlockSpec(memory_space=pltpu.VMEM),) * 3,
        scratch_shapes=scratch,
        compiler_params=pltpu.CompilerParams(
            collective_id=0, has_side_effects=True, vmem_limit_bytes=VMEM_LIMIT
        ),
    )(acts, before, upper, weights)


def store(grad_in, wide_in, bias_in, grad_out, wide_out, bias_out, sems):
    pair, _, share, _ = wide_in.shape
    copies = [
        pltpu.make_async_copy(
            wide_in.at[side, pl.ds(0, wide_out.shape[0])],
            wide_out.at[:, pl.ds(side * share, share)],
            sems.at[2 + side],
        )
        for side in range(pair)
    ]
    copies.append(pltpu.make_async_copy(grad_in, grad_out, sems.at[0]))
    copies.append(pltpu.make_async_copy(bias_in, bias_out, sems.at[1]))
    for copy in copies:
        copy.start()
    for copy in copies:
        copy.wait()


def finish(grad, wide, bias, offsets):
    pair, _, share, chan_out = wide.shape
    return pl.pallas_call(
        store,
        out_shape=(
            jax.ShapeDtypeStruct(grad.shape, grad.dtype),
            jax.ShapeDtypeStruct((offsets, pair * share, chan_out), wide.dtype),
            jax.ShapeDtypeStruct(bias.shape, bias.dtype),
        ),
        in_specs=[pl.BlockSpec(memory_space=pltpu.VMEM)] * 3,
        out_specs=(pl.BlockSpec(memory_space=pltpu.MemorySpace.HBM),) * 3,
        scratch_shapes=[pltpu.SemaphoreType.DMA((2 + pair,))],
        compiler_params=pltpu.CompilerParams(vmem_limit_bytes=STORE_LIMIT),
    )(grad, wide, bias)


def fold(array):
    rows, cols, flat = array.shape
    array = array.reshape(rows, cols, flat // LANES, LANES).transpose(0, 2, 1, 3)
    return array.reshape(rows, flat // LANES * cols, LANES)


def on_device(sizes, activations, preact, pooled_grad, weights):
    samples, cells_x, cells_y, _ = activations.shape
    offsets, chan_in, chan_out = weights.shape
    acts = fold(activations.reshape(activations.shape[1:]))
    before = fold(preact.reshape(preact.shape[1:]))
    upper = fold(pooled_grad.reshape(pooled_grad.shape[1:]))
    grad, total, bias = fused(acts, before, upper, weights, cells_y, samples, sizes)
    pair = span("core", sizes)
    total = total.reshape(pair, -1, chan_in // pair, chan_out)
    grad, total, bias = finish(grad, total, bias, offsets)
    grad = grad.reshape(cells_x, -1, cells_y, LANES).transpose(0, 2, 1, 3)
    return (
        grad.reshape(activations.shape),
        total,
        bias.reshape(chan_out),
    )


def solution(mesh):
    sizes = tuple(mesh.shape[axis] for axis in AXES)
    placed = (P("dp", "sx", "sy", None), P("dp", "sx", "sy", None), P("dp", "sx", "sy", None), P())
    return jax.shard_map(
        functools.partial(on_device, sizes),
        mesh=mesh,
        in_specs=placed,
        out_specs=(P("dp", "sx", "sy", None), P(), P()),
        check_vma=False,
    )
```

```python
import functools
import itertools
import math

import jax
import jax.numpy as jnp
from jax import lax
from jax.experimental import pallas as pl
from jax.experimental.pallas import tpu as pltpu
from jax.sharding import PartitionSpec as P

MESH = pl.DeviceIdType.MESH
AXES = ("dp", "sx", "sy")
ROWS = 8
LANES = 128
FACTORS = ("core", "chip", "sx", "sy")
CODE = 2.0**36
ONE_SHOT = 16
PARTS = 4
NEAR = 2
VMEM_LIMIT = 56 * 1024 * 1024
STORE_LIMIT = 8 * 1024 * 1024


def span(name, sizes):
    pair = 2 if sizes[0] % 2 == 0 else 1
    return {"core": pair, "chip": sizes[0] // pair, "sx": sizes[1], "sy": sizes[2]}[name]


def plan_stages(sizes):
    rest = span("chip", sizes) * sizes[1] * sizes[2]
    groups = [("chip", "sx", "sy")] if rest <= ONE_SHOT else [("chip",), ("sx",), ("sy",)]
    stages = []
    for group in groups:
        count = 1
        for name in group:
            count *= span(name, sizes)
        if count > 1:
            stages.append((group, count))
    return stages


def digits(sizes, group):
    found = []
    for name in group:
        left = span(name, sizes)
        while left % 2 == 0:
            found.append(2)
            left //= 2
        if left > 1:
            found.append(left)
    return found


def moved(radices, index, move, way=1):
    result, weight = 0, 1
    for radix in reversed(radices):
        result = result + (index % radix + way * (move % radix) + radix) % radix * weight
        index, move, weight = index // radix, move // radix, weight * radix
    return result


def reach(sizes, group, here):
    values = split(sizes, here)
    ahead, behind = {}, {}
    for name in group:
        radices = digits(sizes, (name,))
        many = range(span(name, sizes))
        ahead[name] = [moved(radices, values[name], move) for move in many]
        behind[name] = ahead[name]
        if any(radix > 2 for radix in radices):
            behind[name] = [moved(radices, values[name], move, -1) for move in many]
    weights, weight = {}, 1
    for name in reversed(group):
        weights[name] = weight
        weight *= span(name, sizes)
    to, origin, device = [], [], []
    terms = {name: [value * weights[name] for value in ahead[name]] for name in group}
    terms_back = terms
    if any(behind[name] is not ahead[name] for name in group):
        terms_back = {name: [value * weights[name] for value in behind[name]] for name in group}
    pair = span("core", sizes)
    chips = [chip * pair + values["core"] for chip in ahead.get("chip", [values["chip"]])]
    for move in range(weight):
        at = {}
        for name in reversed(group):
            at[name] = move // weights[name] % span(name, sizes)
        to.append(sum(terms[name][at[name]] for name in group))
        origin.append(sum(terms_back[name][at[name]] for name in group))
        device.append(
            (
                chips[at.get("chip", 0)],
                ahead["sx"][at["sx"]] if "sx" in at else values["sx"],
                ahead["sy"][at["sy"]] if "sy" in at else values["sy"],
            )
        )
    return to, origin, device


def moves_of(sizes, group, way):
    count = 1
    for name in group:
        count *= span(name, sizes)

    def steps(move):
        total = 0
        for name in reversed(group):
            size = span(name, sizes)
            total += move % size
            move //= size
        return way * total

    return sorted(range(1, count), key=steps)


def place():
    return tuple(lax.axis_index(axis) for axis in AXES)


def split(sizes, here):
    d, x, y = here
    pair = span("core", sizes)
    return {"core": d % pair, "chip": d // pair, "sx": x, "sy": y}


def encode(value):
    scaled = value * CODE
    return (scaled * jnp.abs(scaled)).astype(jnp.bfloat16)


def decode(coded):
    wide = coded.astype(jnp.float32)
    root = jnp.sqrt(jnp.abs(wide)) * (1.0 / CODE)
    return jnp.where(wide < 0, -root, root)


def body(sizes, stages, chunks, samples, acts_hbm, pre_hbm, pool_hbm, weights_hbm,
         grad_ref, wide_ref, bias_ref, *scratch):
    (acts_in, pre_in, pool_in, weights_ref, acts_wide, pre_wide, pool_wide, planes, far,
     row_out, row_in, col_out, col_in,
     turned, taps, acc, total, landing, leaving, load_sem, halo_send, halo_recv,
     pair_send, pair_recv, red_send, red_recv, gat_send, gat_recv, fwd_send, fwd_recv) = scratch
    loads = [
        pltpu.make_async_copy(src, dst, load_sem.at[n])
        for n, (src, dst) in enumerate(
            ((acts_hbm, acts_in), (pre_hbm, pre_in), (pool_hbm, pool_in), (weights_hbm, weights_ref))
        )
    ]
    for load in loads[:3]:
        load.start()
    here = place()
    d, x, y = here
    pair = span("core", sizes)
    core = d % pair
    mate = d + 1 - 2 * core if pair == 2 else d
    cells_x = acts_in.shape[0]
    cells_y, deep = planes.shape[2] - 2, planes.shape[4]
    offsets, chan_in, chan_out = weights_hbm.shape
    share = chan_in // pair
    plane = cells_x * deep
    cells = cells_y * plane
    units = share // ROWS
    bias_unit = offsets * units
    depth = len(stages)
    routes = [reach(sizes, group, here) for group, _ in stages]
    ways = [(0, -1), (0, 1), (-1, 0), (1, 0), (-1, -1), (-1, 1), (1, -1), (1, 1)]

    def inside(dx, dy):
        ok = None
        for coord, step, size in ((x, dx, sizes[1]), (y, dy, sizes[2])):
            if step == -1:
                term = coord > 0
            elif step == 1:
                term = coord < size - 1
            else:
                continue
            ok = term if ok is None else jnp.logical_and(ok, term)
        return ok

    barrier = pltpu.get_barrier_semaphore()
    greeted = 0

    def greet(target):
        pl.semaphore_signal(barrier, inc=1, device_id=target, device_id_type=MESH)

    if pair == 2:
        greet((mate, x, y))
        greeted += 1
    for (group, _), (_, _, device) in zip(stages, routes):
        for move in moves_of(sizes, group, -1):
            greet(device[move])
            greeted += 1
    known = any(group == ("chip", "sx", "sy") for group, _ in stages)
    for dx, dy in ways:
        @pl.when(inside(dx, dy))
        def _():
            if pair == 2:
                greet((mate, x + dx, y + dy))
            if not known:
                greet((d, x + dx, y + dy))
    for dx, dy in ways:
        greeted = greeted + jnp.where(inside(dx, dy), pair - 1 + (0 if known else 1), 0)

    def edge(step, size):
        return pl.ds(1, size) if step == 0 else (1 if step == -1 else size)

    def rim(step, size):
        return pl.ds(1, size) if step == 0 else (0 if step == -1 else size + 1)

    def lane_of(dx, dy):
        near_x, near_y = (abs(dx) if sizes[1] <= 2 else dx), (abs(dy) if sizes[2] <= 2 else dy)
        return ways.index((near_x, near_y)) if (near_x or near_y) else 0

    used = sorted({lane_of(dx, dy) for dx, dy in ways})

    def packed(dx, dy):
        return pair == 2 and (dx == 0 or dy == 0)

    def swapped(value, to_side):
        low, high = pltpu.roll(value, share, 2), pltpu.roll(value, LANES - share, 2)
        return jnp.where(to_side == 0, low, high)

    def pack(edge_cells, out, side):
        wide = edge_cells.astype(jnp.float32)
        half = wide.shape[0] // 2
        lane = lax.broadcasted_iota(jnp.int32, (half, deep, LANES), 2)
        for slot in (0, 1):
            to_side = core if slot == 0 else 1 - core
            value = jnp.where(
                (lane // share) % 2 == to_side, wide[:half], swapped(wide[half:], to_side)
            )
            out[side, slot] = value.astype(jnp.bfloat16)

    def unpack(dx, dy):
        land = row_in if dx == 0 else col_in
        for slot in (0, 1):
            first = land[(dx + dy + 1) // 2, slot]
            second = swapped(first.astype(jnp.float32), 1 - core).astype(jnp.bfloat16)
            ref = planes.at[slot, 0, rim(dy, cells_y), rim(dx, cells_x)]
            ref[...] = jnp.concatenate([first, second], axis=0)

    def halo_copy(kind, slot, dx, dy):
        if kind == 0 and packed(dx, dy):
            out, land = (row_out, row_in) if dx == 0 else (col_out, col_in)
            side = (dx + dy + 1) // 2
            src, dst = out.at[side, slot], land.at[1 - side, slot]
        else:
            kinds = 0 if kind == 0 else pl.ds(1, 2)
            src = planes.at[0, kinds, edge(dy, cells_y), edge(dx, cells_x)]
            dst = planes.at[slot, kinds, rim(-dy, cells_y), rim(-dx, cells_x)]
        return pltpu.make_async_remote_copy(
            src_ref=src,
            dst_ref=dst,
            send_sem=halo_send.at[used.index(lane_of(dx, dy))],
            recv_sem=halo_recv.at[kind, used.index(lane_of(-dx, -dy))],
            device_id=(mate if slot else d, x + dx, y + dy),
            device_id_type=MESH,
        )

    def whole(ref, send_sem, recv_sem):
        return pltpu.make_async_remote_copy(
            src_ref=ref, dst_ref=ref, send_sem=send_sem, recv_sem=recv_sem,
            device_id=(mate, x, y), device_id_type=MESH,
        )

    def halo_arrived(kind):
        for dx, dy in ways:
            @pl.when(inside(dx, dy))
            def _():
                where = (rim(dy, cells_y), rim(dx, cells_x))
                if kind:
                    ref = planes.at[0, pl.ds(1, 2), *where]
                elif packed(dx, dy):
                    ref = (row_in if dx == 0 else col_in).at[(dx + dy + 1) // 2]
                else:
                    ref = planes.at[:, 0, *where]
                n = used.index(lane_of(dx, dy))
                whole(ref, halo_send.at[n], halo_recv.at[kind, n]).wait_recv()
                if kind == 0 and packed(dx, dy):
                    unpack(dx, dy)

    def halo_left():
        for dx, dy in ways:
            @pl.when(inside(dx, dy))
            def _():
                where = (edge(dy, cells_y), edge(dx, cells_x))
                ref = planes.at[0, :, *where]
                if pair == 2 and not packed(dx, dy):
                    ref = planes.at[:, pl.ds(0, 2), *where]
                n = used.index(lane_of(dx, dy))
                whole(ref, halo_send.at[n], halo_recv.at[0, n]).wait_send()

    def send_halo(kind):
        for dx, dy in ways:
            @pl.when(inside(dx, dy))
            def _():
                halo_copy(kind, 0, dx, dy).start()
                if kind == 0 and pair == 2:
                    halo_copy(kind, 1, dx, dy).start()

    inner = (pl.ds(1, cells_y), pl.ds(1, cells_x))

    def pair_copy(kind):
        kinds = pl.ds(0, 1) if kind == 0 else pl.ds(1, 2)
        return pltpu.make_async_remote_copy(
            src_ref=planes.at[0, kinds, *inner],
            dst_ref=planes.at[1, kinds, *inner],
            send_sem=pair_send.at[0],
            recv_sem=pair_recv.at[kind],
            device_id=(mate, x, y),
            device_id_type=MESH,
        )

    for dx, dy in ways:
        @pl.when(jnp.logical_not(inside(dx, dy)))
        def _():
            where = (rim(dy, cells_y), rim(dx, cells_x))
            for ref in [planes.at[0, n, *where] for n in range(3)] + [
                planes.at[slot, 0, *where] for slot in range(1, pair)
            ]:
                ref[...] = jnp.zeros(ref.shape, jnp.bfloat16)

    loads[0].wait()
    acts_wide[...] = acts_in[...].astype(jnp.float32).reshape(acts_wide.shape)
    for row in range(cells_y):
        planes[0, 0, 1 + row, pl.ds(1, cells_x)] = (
            acts_wide[pl.ds(row, plane, stride=cells_y), :]
            .astype(jnp.bfloat16)
            .reshape(cells_x, deep, LANES)
        )
    if pair == 2:
        for side in (0, 1):
            pack(planes[0, 0, 1 + side * (cells_y - 1), inner[1]], row_out, side)
            pack(planes[0, 0, inner[0], 1 + side * (cells_x - 1)], col_out, side)
    pl.semaphore_wait(barrier, greeted)
    send_halo(0)
    if pair == 2:
        pair_copy(0).start()
    loads[1].wait()
    loads[2].wait()
    loads[3].start()
    pre_wide[...] = pre_in[...].astype(jnp.float32).reshape(pre_wide.shape)
    pool_wide[...] = pool_in[...].astype(jnp.float32).reshape(pool_wide.shape) * 0.125
    for half in range(cells_y // 2):
        upper = pool_wide[pl.ds(half, plane // 2, stride=cells_y // 2), :]
        upper = jnp.broadcast_to(
            upper.reshape(cells_x // 2, 1, deep, LANES), (cells_x // 2, 2, deep, LANES)
        ).reshape(plane, LANES)
        for row in (2 * half, 2 * half + 1):
            for odd in (0, 1):
                before = pre_wide[pl.ds(odd * cells_y + row, plane, stride=2 * cells_y), :]
                gate = (upper * jnp.where(before > 0, 1.0, 0.3)).astype(jnp.bfloat16)
                planes[0, 1 + odd, 1 + row, pl.ds(1, cells_x)] = gate.reshape(cells_x, deep, LANES)
    if pair == 2:
        pair_copy(1).start()
    send_halo(1)

    def shift_z(slot, odd, rows, cols):
        wide = planes[slot, 1 + odd, rows, cols].astype(jnp.float32)
        axis = wide.ndim - 2
        depth_z = lax.broadcasted_iota(jnp.int32, wide.shape, axis)
        if odd:
            away = jnp.where(depth_z == 0, 0.0, pltpu.roll(wide, 1, axis))
        else:
            away = jnp.where(depth_z == deep - 1, 0.0, pltpu.roll(wide, deep - 1, axis))
        far[slot, odd, rows, cols] = away.astype(jnp.bfloat16)

    def turn_planes(slot, rows, a_all):
        for row in rows:
            for a in a_all:
                piece = planes[slot, 0, row, pl.ds(1 + a, cells_x)].reshape(plane, LANES)
                turned[slot, 1 + a, :, pl.ds(row * plane, plane)] = piece.T

    bias = jnp.zeros((ROWS, chan_out), jnp.float32)
    middle = range(1, 1 + cells_y)
    for slot in range(pair):
        if slot:
            for kind in (0, 1):
                pair_copy(kind).wait_recv()
        for odd in (0, 1):
            for row in middle:
                shift_z(slot, odd, row, pl.ds(1, cells_x))
                wide = planes[slot, 1 + odd, row, pl.ds(1, cells_x)].astype(jnp.float32)
                bias = bias + jnp.sum(wide.reshape(-1, ROWS, chan_out), axis=0)
        turn_planes(slot, middle, (0,))
    bias = jnp.sum(bias, axis=0, keepdims=True)
    top = lax.broadcasted_iota(jnp.int32, (ROWS, chan_out), 0) == 0
    acc[bias_unit] = jnp.where(top, jnp.broadcast_to(bias, (ROWS, chan_out)), 0.0)
    spare = acc.shape[0] - bias_unit - 1
    if spare:
        acc[pl.ds(bias_unit + 1, spare)] = jnp.zeros((spare, ROWS, chan_out), jnp.float32)

    halo_arrived(0)
    for slot in range(pair):
        turn_planes(slot, range(cells_y + 2), (-1, 1))
        turn_planes(slot, (0, cells_y + 1), (0,))

    def flat(ref, slot, odd):
        return ref[slot, odd, inner[0], inner[1]].reshape(cells, LANES)

    term = None
    for slot in range(pair):
        for odd in (0, 1):
            if odd:
                kinds = ((far, 0), (planes, 2), (planes, 1))
            else:
                kinds = ((planes, 2), (planes, 1), (far, 1))
            rhs = jnp.concatenate([flat(ref, slot, n) for ref, n in kinds], axis=1)
            rows = pl.ds(pl.multiple_of(odd * chan_in + core * share, share), share)
            lhs = jnp.concatenate(
                [
                    turned[slot, a, rows, pl.ds(b * plane, cells)]
                    for a in range(3)
                    for b in range(3)
                ],
                axis=0,
            )
            piece = jnp.dot(lhs, rhs, preferred_element_type=jnp.float32)
            term = piece if term is None else term + piece
    for n in range(offsets // 3):
        for c in range(3):
            acc[pl.ds((3 * n + c) * units, units)] = term[
                n * share : (n + 1) * share, c * chan_out : (c + 1) * chan_out
            ].reshape(units, ROWS, chan_out)

    starts = [0]

    def span_of(stage, index):
        return pl.ds(starts[stage] + index * chunks[stage], chunks[stage])

    def offset_of(stage):
        return sum((stages[s][1] - 1) * chunks[s] for s in range(stage))

    def arrivals(stage):
        return pl.ds(offset_of(stage), (stages[stage][1] - 1) * chunks[stage])

    def at_last(target, name, last):
        if name == "chip":
            return (last * pair + core,) + target[1:]
        return target[:1] + ((last, target[2]) if name == "sx" else (target[1], last))

    def send_reduce(stage):
        group, count = stages[stage]
        chunk = chunks[stage]
        to, _, device = routes[stage]
        rows = pl.ds(starts[stage], count * chunk)
        leaving[rows] = encode(acc[rows])
        name = group[-1]
        deep_last = span(name, sizes)
        own_last = split(sizes, here)[name]
        for last in [k for k in reversed(range(deep_last)) if k % 2] + [k for k in reversed(range(deep_last)) if k % 2 == 0]:
            step = (last - own_last + deep_last) % deep_last
            for first in reversed(range(0, count, deep_last)):
                index = to[first] - own_last + last
                copy = pltpu.make_async_remote_copy(
                    src_ref=leaving.at[span_of(stage, index)],
                    dst_ref=landing.at[pl.ds(offset_of(stage) + (first + step - 1) * chunk, chunk)],
                    send_sem=red_send.at[stage],
                    recv_sem=red_recv.at[stage],
                    device_id=at_last(device[first], name, last),
                    device_id_type=MESH,
                )
                if first:
                    copy.start()
                else:
                    pl.when(own_last != last)(copy.start)

    def take_reduce(stage):
        group, count = stages[stage]
        chunk = chunks[stage]
        own = starts[stage] + routes[stage][0][0] * chunk
        value = acc[pl.ds(own, chunk)]
        copies = whole(landing.at[arrivals(stage)], red_send.at[stage], red_recv.at[stage])
        copies.wait_recv()
        for turn in range(count - 1):
            value = value + decode(landing[pl.ds(offset_of(stage) + turn * chunk, chunk)])
        copies.wait_send()
        acc[pl.ds(own, chunk)] = value
        starts.append(own)

    def make_taps():
        loads[3].wait()
        blank = jnp.zeros((chan_in, chan_out), jnp.bfloat16)
        for n in range(offsets // 3):
            three = [weights_ref[3 * n + c] for c in range(3)]
            taps[n, pl.ds(0, chan_in)] = jnp.concatenate([blank] + three, axis=1)
            taps[n, pl.ds(chan_in, chan_in)] = jnp.concatenate(three + [blank], axis=1)

    def input_gradient():
        make_taps()
        halo_arrived(1)
        for odd in (0, 1):
            for row in (0, cells_y + 1):
                shift_z(0, odd, row, pl.ds(0, cells_x + 2))
            for col in (0, cells_x + 1):
                shift_z(0, odd, pl.ds(1, cells_y), col)
        sums = None
        for a in (-1, 0, 1):
            for b in (-1, 0, 1):
                ys, xs = pl.ds(1 - b, cells_y), pl.ds(1 - a, cells_x)
                lhs = jnp.concatenate(
                    [
                        ref[0, n, ys, xs].reshape(cells, LANES)
                        for ref, n in ((far, 0), (planes, 2), (planes, 1), (far, 1))
                    ],
                    axis=1,
                )
                piece = lax.dot_general(
                    lhs,
                    taps[3 * (a + 1) + b + 1],
                    (((1,), (1,)), ((), ())),
                    preferred_element_type=jnp.float32,
                )
                sums = piece if sums is None else sums + piece
        for row in range(cells_y):
            acts_wide[pl.ds(row, plane, stride=cells_y), :] = sums[row * plane : (row + 1) * plane]
        grad_ref[...] = acts_wide[...].astype(jnp.bfloat16).reshape(grad_ref.shape)

    for stage in range(depth):
        send_reduce(stage)
        if stage == 0:
            input_gradient()
        take_reduce(stage)

    own, chunk = starts[-1], chunks[-1]
    value = acc[pl.ds(own, chunk)] * (1.0 / (samples * sizes[0]))
    coded = encode(value)
    rest = pltpu.roll(value - decode(coded), 1, 1)
    unit = own + lax.broadcasted_iota(jnp.int32, value.shape, 0)
    row = lax.broadcasted_iota(jnp.int32, value.shape, 1)
    is_rest = jnp.logical_and(unit == bias_unit, row == 1)
    total[core, pl.ds(own, chunk)] = encode(jnp.where(is_rest, rest, value))

    def unfold(side, rows):
        wide_ref[side, rows] = decode(total[side, rows])

    def forward(part, rows):
        ref = total.at[core, rows]
        pltpu.make_async_remote_copy(
            src_ref=ref, dst_ref=ref, send_sem=fwd_send.at[0], recv_sem=fwd_recv.at[part],
            device_id=(mate, x, y), device_id_type=MESH,
        ).start()

    for stage in reversed(range(depth)):
        group, count = stages[stage]
        to, origin, device = routes[stage]
        me = to[0]
        ref = total.at[core, span_of(stage, me)]
        name = group[-1]
        deep_last = span(name, sizes)
        own_last = split(sizes, here)[name]
        firsts = list(reversed(range(0, count, deep_last)))
        nearby = {first: 0 for first in firsts}
        if len(group) > 1:
            nearby = {first: device[first][0] // pair + device[first][1] for first in firsts}
        for rank, first, last in itertools.product(range(NEAR + 1), firsts, range(deep_last)):
            if last > rank and rank < NEAR:
                continue
            copy = pltpu.make_async_remote_copy(
                src_ref=ref, dst_ref=ref, send_sem=gat_send.at[stage],
                recv_sem=gat_recv.at[stage * PARTS + first // deep_last],
                device_id=at_last(device[first], name, last), device_id_type=MESH,
            )
            steps = nearby[first] + last
            ok = (steps == rank) if rank < NEAR else (steps >= rank)
            if not first:
                ok = jnp.logical_and(ok, own_last != last)
            pl.when(ok)(copy.start)

        def sources(first):
            return [
                origin[first] - own_last + (own_last + turn) % deep_last
                for turn in range(0 if first else 1, deep_last)
            ]

        last = stage == 0
        if last and pair == 2:
            forward(0, span_of(stage, me))
        if stage == depth - 1:
            unfold(core, span_of(stage, me))
        for first in reversed(firsts):
            part = first // deep_last
            origins = sources(first)
            if not origins:
                continue
            ref = total.at[0, pl.ds(0, len(origins) * chunks[stage])]
            whole(ref, gat_send.at[stage], gat_recv.at[stage * PARTS + part]).wait_recv()
            if last and pair == 2:
                for index in origins:
                    forward(1 + part, span_of(stage, index))
            for index in origins:
                unfold(core, span_of(stage, index))
    if pair == 2:
        for part in range(len(firsts) + 1):
            origins = sources((part - 1) * deep_last) if part else [me]
            if not origins:
                continue
            ref = total.at[0, pl.ds(0, len(origins) * chunks[0])]
            whole(ref, fwd_send.at[0], fwd_recv.at[part]).wait_recv()
            for index in origins:
                unfold(1 - core, span_of(0, index))
    bias_ref[...] = wide_ref[0, bias_unit, pl.ds(0, 1)] + wide_ref[0, bias_unit, pl.ds(1, 1)]
    for stage in range(depth):
        ref = total.at[0, pl.ds(0, (stages[stage][1] - 1) * chunks[stage])]
        whole(ref, gat_send.at[stage], gat_recv.at[stage * PARTS]).wait_send()
    if pair == 2:
        whole(total.at[0], fwd_send.at[0], fwd_recv.at[0]).wait_send()
        ref = planes.at[0, :, *inner]
        whole(ref, pair_send.at[0], pair_recv.at[0]).wait_send()
    halo_left()


def fused(acts, before, upper, weights, cells_y, samples, sizes):
    cells_x, rows_acts, _ = acts.shape
    deep = rows_acts // cells_y
    offsets, chan_in, chan_out = weights.shape
    stages = plan_stages(sizes)
    pair = span("core", sizes)
    devices = 1
    for _, count in stages:
        devices *= count
    per_tap = chan_in // pair // ROWS
    step = math.lcm(devices, per_tap)
    units = -(-(offsets * per_tap + 1) // step) * step
    chunks = []
    for _, count in stages:
        chunks.append((chunks[-1] if chunks else units) // count)
    arriving = sum((count - 1) * chunk for (_, count), chunk in zip(stages, chunks))
    half, full = jnp.bfloat16, jnp.float32
    padded = (cells_y + 2, cells_x + 2, deep, LANES)
    cells = cells_x * rows_acts
    dma = pltpu.SemaphoreType.DMA
    lanes = (2 if sizes[1] <= 2 else 3) * (2 if sizes[2] <= 2 else 3) - 1
    scratch = [
        pltpu.VMEM(acts.shape, half),
        pltpu.VMEM(before.shape, half),
        pltpu.VMEM(upper.shape, half),
        pltpu.VMEM(weights.shape, half),
        pltpu.VMEM((cells, LANES), full),
        pltpu.VMEM((2 * cells, LANES), full),
        pltpu.VMEM((upper.shape[0] * upper.shape[1], LANES), full),
        pltpu.VMEM((pair, 3) + padded, half),
        pltpu.VMEM((pair, 2) + padded, half),
        pltpu.VMEM((2, pair, cells_x // 2, deep, LANES), half),
        pltpu.VMEM((2, pair, cells_x // 2, deep, LANES), half),
        pltpu.VMEM((2, pair, cells_y // 2, deep, LANES), half),
        pltpu.VMEM((2, pair, cells_y // 2, deep, LANES), half),
        pltpu.VMEM((pair, 3, LANES, (cells_y + 2) * cells_x * deep), half),
        pltpu.VMEM((offsets // 3, LANES, 4 * chan_out), half),
        pltpu.VMEM((units, ROWS, chan_out), full),
        pltpu.VMEM((pair, units, ROWS, chan_out), half),
        pltpu.VMEM((arriving, ROWS, chan_out), half),
        pltpu.VMEM((units, ROWS, chan_out), half),
        dma((4,)),
        dma((lanes,)),
        dma((2, lanes)),
        dma((1,)),
        dma((2,)),
        dma((len(stages),)),
        dma((len(stages),)),
        dma((len(stages),)),
        dma((len(stages) * PARTS,)),
        dma((1,)),
        dma((PARTS + 1,)),
    ]
    return pl.pallas_call(
        functools.partial(body, sizes, stages, chunks, samples),
        out_shape=(
            pltpu.VMEM(acts.shape, half),
            pltpu.VMEM((pair, units, ROWS, chan_out), full),
            pltpu.VMEM((1, chan_out), full),
        ),
        in_specs=[pl.BlockSpec(memory_space=pltpu.MemorySpace.HBM)] * 4,
        out_specs=(pl.BlockSpec(memory_space=pltpu.VMEM),) * 3,
        scratch_shapes=scratch,
        compiler_params=pltpu.CompilerParams(
            collective_id=0, has_side_effects=True, vmem_limit_bytes=VMEM_LIMIT
        ),
    )(acts, before, upper, weights)


def store(grad_in, wide_in, bias_in, grad_out, wide_out, bias_out, sems):
    pair, _, share, _ = wide_in.shape
    copies = [
        pltpu.make_async_copy(
            wide_in.at[side, pl.ds(0, wide_out.shape[0])],
            wide_out.at[:, pl.ds(side * share, share)],
            sems.at[2 + side],
        )
        for side in range(pair)
    ]
    copies.append(pltpu.make_async_copy(grad_in, grad_out, sems.at[0]))
    copies.append(pltpu.make_async_copy(bias_in, bias_out, sems.at[1]))
    for copy in copies:
        copy.start()
    for copy in copies:
        copy.wait()


def finish(grad, wide, bias, offsets):
    pair, _, share, chan_out = wide.shape
    return pl.pallas_call(
        store,
        out_shape=(
            jax.ShapeDtypeStruct(grad.shape, grad.dtype),
            jax.ShapeDtypeStruct((offsets, pair * share, chan_out), wide.dtype),
            jax.ShapeDtypeStruct(bias.shape, bias.dtype),
        ),
        in_specs=[pl.BlockSpec(memory_space=pltpu.VMEM)] * 3,
        out_specs=(pl.BlockSpec(memory_space=pltpu.MemorySpace.HBM),) * 3,
        scratch_shapes=[pltpu.SemaphoreType.DMA((2 + pair,))],
        compiler_params=pltpu.CompilerParams(vmem_limit_bytes=STORE_LIMIT),
    )(grad, wide, bias)


def fold(array):
    rows, cols, flat = array.shape
    array = array.reshape(rows, cols, flat // LANES, LANES).transpose(0, 2, 1, 3)
    return array.reshape(rows, flat // LANES * cols, LANES)


def on_device(sizes, activations, preact, pooled_grad, weights):
    samples, cells_x, cells_y, _ = activations.shape
    offsets, chan_in, chan_out = weights.shape
    acts = fold(activations.reshape(activations.shape[1:]))
    before = fold(preact.reshape(preact.shape[1:]))
    upper = fold(pooled_grad.reshape(pooled_grad.shape[1:]))
    grad, total, bias = fused(acts, before, upper, weights, cells_y, samples, sizes)
    pair = span("core", sizes)
    total = total.reshape(pair, -1, chan_in // pair, chan_out)
    grad, total, bias = finish(grad, total, bias, offsets)
    grad = grad.reshape(cells_x, -1, cells_y, LANES).transpose(0, 2, 1, 3)
    return (
        grad.reshape(activations.shape),
        total,
        bias.reshape(chan_out),
    )


def solution(mesh):
    sizes = tuple(mesh.shape[axis] for axis in AXES)
    placed = (P("dp", "sx", "sy", None), P("dp", "sx", "sy", None), P("dp", "sx", "sy", None), P())
    return jax.shard_map(
        functools.partial(on_device, sizes),
        mesh=mesh,
        in_specs=placed,
        out_specs=(P("dp", "sx", "sy", None), P(), P()),
        check_vma=False,
    )
```

```python
import functools
import itertools
import math

import jax
import jax.numpy as jnp
from jax import lax
from jax.experimental import pallas as pl
from jax.experimental.pallas import tpu as pltpu
from jax.sharding import PartitionSpec as P

MESH = pl.DeviceIdType.MESH
AXES = ("dp", "sx", "sy")
ROWS = 8
LANES = 128
FACTORS = ("core", "chip", "sx", "sy")
CODE = 2.0**36
ONE_SHOT = 16
PARTS = 4
NEAR = 2
VMEM_LIMIT = 56 * 1024 * 1024
STORE_LIMIT = 8 * 1024 * 1024


def span(name, sizes):
    pair = 2 if sizes[0] % 2 == 0 else 1
    return {"core": pair, "chip": sizes[0] // pair, "sx": sizes[1], "sy": sizes[2]}[name]


def plan_stages(sizes):
    rest = span("chip", sizes) * sizes[1] * sizes[2]
    groups = [("chip", "sx", "sy")] if rest <= ONE_SHOT else [("chip",), ("sx",), ("sy",)]
    stages = []
    for group in groups:
        count = 1
        for name in group:
            count *= span(name, sizes)
        if count > 1:
            stages.append((group, count))
    return stages


def digits(sizes, group):
    found = []
    for name in group:
        left = span(name, sizes)
        while left % 2 == 0:
            found.append(2)
            left //= 2
        if left > 1:
            found.append(left)
    return found


def moved(radices, index, move, way=1):
    result, weight = 0, 1
    for radix in reversed(radices):
        result = result + (index % radix + way * (move % radix) + radix) % radix * weight
        index, move, weight = index // radix, move // radix, weight * radix
    return result


def reach(sizes, group, here):
    values = split(sizes, here)
    ahead, behind = {}, {}
    for name in group:
        radices = digits(sizes, (name,))
        many = range(span(name, sizes))
        ahead[name] = [moved(radices, values[name], move) for move in many]
        behind[name] = ahead[name]
        if any(radix > 2 for radix in radices):
            behind[name] = [moved(radices, values[name], move, -1) for move in many]
    weights, weight = {}, 1
    for name in reversed(group):
        weights[name] = weight
        weight *= span(name, sizes)
    to, origin, device = [], [], []
    terms = {name: [value * weights[name] for value in ahead[name]] for name in group}
    terms_back = terms
    if any(behind[name] is not ahead[name] for name in group):
        terms_back = {name: [value * weights[name] for value in behind[name]] for name in group}
    pair = span("core", sizes)
    chips = [chip * pair + values["core"] for chip in ahead.get("chip", [values["chip"]])]
    for move in range(weight):
        at = {}
        for name in reversed(group):
            at[name] = move // weights[name] % span(name, sizes)
        to.append(sum(terms[name][at[name]] for name in group))
        origin.append(sum(terms_back[name][at[name]] for name in group))
        device.append(
            (
                chips[at.get("chip", 0)],
                ahead["sx"][at["sx"]] if "sx" in at else values["sx"],
                ahead["sy"][at["sy"]] if "sy" in at else values["sy"],
            )
        )
    return to, origin, device


def moves_of(sizes, group, way):
    count = 1
    for name in group:
        count *= span(name, sizes)

    def steps(move):
        total = 0
        for name in reversed(group):
            size = span(name, sizes)
            total += move % size
            move //= size
        return way * total

    return sorted(range(1, count), key=steps)


def place():
    return tuple(lax.axis_index(axis) for axis in AXES)


def split(sizes, here):
    d, x, y = here
    pair = span("core", sizes)
    return {"core": d % pair, "chip": d // pair, "sx": x, "sy": y}


def encode(value):
    scaled = value * CODE
    return (scaled * jnp.abs(scaled)).astype(jnp.bfloat16)


def decode(coded):
    wide = coded.astype(jnp.float32)
    root = jnp.sqrt(jnp.abs(wide)) * (1.0 / CODE)
    return jnp.where(wide < 0, -root, root)


def body(sizes, stages, chunks, samples, acts_hbm, pre_hbm, pool_hbm, weights_hbm,
         grad_ref, wide_ref, bias_ref, *scratch):
    (acts_in, pre_in, pool_in, weights_ref, acts_wide, pre_wide, pool_wide, planes, far,
     row_out, row_in, col_out, col_in,
     turned, taps, acc, total, landing, leaving, load_sem, halo_send, halo_recv,
     pair_send, pair_recv, red_send, red_recv, gat_send, gat_recv, fwd_send, fwd_recv) = scratch
    loads = [
        pltpu.make_async_copy(src, dst, load_sem.at[n])
        for n, (src, dst) in enumerate(
            ((acts_hbm, acts_in), (pre_hbm, pre_in), (pool_hbm, pool_in), (weights_hbm, weights_ref))
        )
    ]
    for load in loads[:3]:
        load.start()
    here = place()
    d, x, y = here
    pair = span("core", sizes)
    core = d % pair
    mate = d + 1 - 2 * core if pair == 2 else d
    cells_x = acts_in.shape[0]
    cells_y, deep = planes.shape[2] - 2, planes.shape[4]
    offsets, chan_in, chan_out = weights_hbm.shape
    share = chan_in // pair
    plane = cells_x * deep
    cells = cells_y * plane
    units = share // ROWS
    bias_unit = offsets * units
    depth = len(stages)
    routes = [reach(sizes, group, here) for group, _ in stages]
    ways = [(0, -1), (0, 1), (-1, 0), (1, 0), (-1, -1), (-1, 1), (1, -1), (1, 1)]

    def inside(dx, dy):
        ok = None
        for coord, step, size in ((x, dx, sizes[1]), (y, dy, sizes[2])):
            if step == -1:
                term = coord > 0
            elif step == 1:
                term = coord < size - 1
            else:
                continue
            ok = term if ok is None else jnp.logical_and(ok, term)
        return ok

    barrier = pltpu.get_barrier_semaphore()
    greeted = 0

    def greet(target):
        pl.semaphore_signal(barrier, inc=1, device_id=target, device_id_type=MESH)

    if pair == 2:
        greet((mate, x, y))
        greeted += 1
    for (group, _), (_, _, device) in zip(stages, routes):
        for move in moves_of(sizes, group, -1):
            greet(device[move])
            greeted += 1
    known = any(group == ("chip", "sx", "sy") for group, _ in stages)
    for dx, dy in ways:
        @pl.when(inside(dx, dy))
        def _():
            if pair == 2:
                greet((mate, x + dx, y + dy))
            if not known:
                greet((d, x + dx, y + dy))
    for dx, dy in ways:
        greeted = greeted + jnp.where(inside(dx, dy), pair - 1 + (0 if known else 1), 0)

    def edge(step, size):
        return pl.ds(1, size) if step == 0 else (1 if step == -1 else size)

    def rim(step, size):
        return pl.ds(1, size) if step == 0 else (0 if step == -1 else size + 1)

    def lane_of(dx, dy):
        near_x, near_y = (abs(dx) if sizes[1] <= 2 else dx), (abs(dy) if sizes[2] <= 2 else dy)
        return ways.index((near_x, near_y)) if (near_x or near_y) else 0

    used = sorted({lane_of(dx, dy) for dx, dy in ways})

    def packed(dx, dy):
        return pair == 2 and (dx == 0 or dy == 0)

    def swapped(value, to_side):
        low, high = pltpu.roll(value, share, 2), pltpu.roll(value, LANES - share, 2)
        return jnp.where(to_side == 0, low, high)

    def pack(edge_cells, out, side):
        wide = edge_cells.astype(jnp.float32)
        half = wide.shape[0] // 2
        lane = lax.broadcasted_iota(jnp.int32, (half, deep, LANES), 2)
        for slot in (0, 1):
            to_side = core if slot == 0 else 1 - core
            value = jnp.where(
                (lane // share) % 2 == to_side, wide[:half], swapped(wide[half:], to_side)
            )
            out[side, slot] = value.astype(jnp.bfloat16)

    def unpack(dx, dy):
        land = row_in if dx == 0 else col_in
        for slot in (0, 1):
            first = land[(dx + dy + 1) // 2, slot]
            second = swapped(first.astype(jnp.float32), 1 - core).astype(jnp.bfloat16)
            ref = planes.at[slot, 0, rim(dy, cells_y), rim(dx, cells_x)]
            ref[...] = jnp.concatenate([first, second], axis=0)

    def halo_copy(kind, slot, dx, dy):
        if kind == 0 and packed(dx, dy):
            out, land = (row_out, row_in) if dx == 0 else (col_out, col_in)
            side = (dx + dy + 1) // 2
            src, dst = out.at[side, slot], land.at[1 - side, slot]
        else:
            kinds = 0 if kind == 0 else pl.ds(1, 2)
            src = planes.at[0, kinds, edge(dy, cells_y), edge(dx, cells_x)]
            dst = planes.at[slot, kinds, rim(-dy, cells_y), rim(-dx, cells_x)]
        return pltpu.make_async_remote_copy(
            src_ref=src,
            dst_ref=dst,
            send_sem=halo_send.at[used.index(lane_of(dx, dy))],
            recv_sem=halo_recv.at[kind, used.index(lane_of(-dx, -dy))],
            device_id=(mate if slot else d, x + dx, y + dy),
            device_id_type=MESH,
        )

    def whole(ref, send_sem, recv_sem):
        return pltpu.make_async_remote_copy(
            src_ref=ref, dst_ref=ref, send_sem=send_sem, recv_sem=recv_sem,
            device_id=(mate, x, y), device_id_type=MESH,
        )

    def halo_arrived(kind):
        for dx, dy in ways:
            @pl.when(inside(dx, dy))
            def _():
                where = (rim(dy, cells_y), rim(dx, cells_x))
                if kind:
                    ref = planes.at[0, pl.ds(1, 2), *where]
                elif packed(dx, dy):
                    ref = (row_in if dx == 0 else col_in).at[(dx + dy + 1) // 2]
                else:
                    ref = planes.at[:, 0, *where]
                n = used.index(lane_of(dx, dy))
                whole(ref, halo_send.at[n], halo_recv.at[kind, n]).wait_recv()
                if kind == 0 and packed(dx, dy):
                    unpack(dx, dy)

    def halo_left():
        for dx, dy in ways:
            @pl.when(inside(dx, dy))
            def _():
                where = (edge(dy, cells_y), edge(dx, cells_x))
                ref = planes.at[0, :, *where]
                if pair == 2 and not packed(dx, dy):
                    ref = planes.at[:, pl.ds(0, 2), *where]
                n = used.index(lane_of(dx, dy))
                whole(ref, halo_send.at[n], halo_recv.at[0, n]).wait_send()

    def send_halo(kind):
        for dx, dy in ways:
            @pl.when(inside(dx, dy))
            def _():
                halo_copy(kind, 0, dx, dy).start()
                if kind == 0 and pair == 2:
                    halo_copy(kind, 1, dx, dy).start()

    inner = (pl.ds(1, cells_y), pl.ds(1, cells_x))

    def pair_copy(kind):
        kinds = pl.ds(0, 1) if kind == 0 else pl.ds(1, 2)
        return pltpu.make_async_remote_copy(
            src_ref=planes.at[0, kinds, *inner],
            dst_ref=planes.at[1, kinds, *inner],
            send_sem=pair_send.at[0],
            recv_sem=pair_recv.at[kind],
            device_id=(mate, x, y),
            device_id_type=MESH,
        )

    for dx, dy in ways:
        @pl.when(jnp.logical_not(inside(dx, dy)))
        def _():
            where = (rim(dy, cells_y), rim(dx, cells_x))
            for ref in [planes.at[0, n, *where] for n in range(3)] + [
                planes.at[slot, 0, *where] for slot in range(1, pair)
            ]:
                ref[...] = jnp.zeros(ref.shape, jnp.bfloat16)

    loads[0].wait()
    acts_wide[...] = acts_in[...].astype(jnp.float32).reshape(acts_wide.shape)
    for row in range(cells_y):
        planes[0, 0, 1 + row, pl.ds(1, cells_x)] = (
            acts_wide[pl.ds(row, plane, stride=cells_y), :]
            .astype(jnp.bfloat16)
            .reshape(cells_x, deep, LANES)
        )
    if pair == 2:
        for side in (0, 1):
            pack(planes[0, 0, 1 + side * (cells_y - 1), inner[1]], row_out, side)
            pack(planes[0, 0, inner[0], 1 + side * (cells_x - 1)], col_out, side)
    pl.semaphore_wait(barrier, greeted)
    send_halo(0)
    if pair == 2:
        pair_copy(0).start()
    loads[1].wait()
    loads[2].wait()
    loads[3].start()
    pre_wide[...] = pre_in[...].astype(jnp.float32).reshape(pre_wide.shape)
    pool_wide[...] = pool_in[...].astype(jnp.float32).reshape(pool_wide.shape) * 0.125
    for half in range(cells_y // 2):
        upper = pool_wide[pl.ds(half, plane // 2, stride=cells_y // 2), :]
        upper = jnp.broadcast_to(
            upper.reshape(cells_x // 2, 1, deep, LANES), (cells_x // 2, 2, deep, LANES)
        ).reshape(plane, LANES)
        for row in (2 * half, 2 * half + 1):
            for odd in (0, 1):
                before = pre_wide[pl.ds(odd * cells_y + row, plane, stride=2 * cells_y), :]
                gate = (upper * jnp.where(before > 0, 1.0, 0.3)).astype(jnp.bfloat16)
                planes[0, 1 + odd, 1 + row, pl.ds(1, cells_x)] = gate.reshape(cells_x, deep, LANES)
    if pair == 2:
        pair_copy(1).start()
    send_halo(1)

    def shift_z(slot, odd, rows, cols):
        wide = planes[slot, 1 + odd, rows, cols].astype(jnp.float32)
        axis = wide.ndim - 2
        depth_z = lax.broadcasted_iota(jnp.int32, wide.shape, axis)
        if odd:
            away = jnp.where(depth_z == 0, 0.0, pltpu.roll(wide, 1, axis))
        else:
            away = jnp.where(depth_z == deep - 1, 0.0, pltpu.roll(wide, deep - 1, axis))
        far[slot, odd, rows, cols] = away.astype(jnp.bfloat16)

    def turn_planes(slot, rows, a_all):
        for row in rows:
            for a in a_all:
                piece = planes[slot, 0, row, pl.ds(1 + a, cells_x)].reshape(plane, LANES)
                turned[slot, 1 + a, :, pl.ds(row * plane, plane)] = piece.T

    bias = jnp.zeros((ROWS, chan_out), jnp.float32)
    middle = range(1, 1 + cells_y)
    for slot in range(pair):
        if slot:
            for kind in (0, 1):
                pair_copy(kind).wait_recv()
        for odd in (0, 1):
            for row in middle:
                shift_z(slot, odd, row, pl.ds(1, cells_x))
                wide = planes[slot, 1 + odd, row, pl.ds(1, cells_x)].astype(jnp.float32)
                bias = bias + jnp.sum(wide.reshape(-1, ROWS, chan_out), axis=0)
        turn_planes(slot, middle, (0,))
    bias = jnp.sum(bias, axis=0, keepdims=True)
    top = lax.broadcasted_iota(jnp.int32, (ROWS, chan_out), 0) == 0
    acc[bias_unit] = jnp.where(top, jnp.broadcast_to(bias, (ROWS, chan_out)), 0.0)
    spare = acc.shape[0] - bias_unit - 1
    if spare:
        acc[pl.ds(bias_unit + 1, spare)] = jnp.zeros((spare, ROWS, chan_out), jnp.float32)

    halo_arrived(0)
    for slot in range(pair):
        turn_planes(slot, range(cells_y + 2), (-1, 1))
        turn_planes(slot, (0, cells_y + 1), (0,))

    def flat(ref, slot, odd):
        return ref[slot, odd, inner[0], inner[1]].reshape(cells, LANES)

    term = None
    for slot in range(pair):
        for odd in (0, 1):
            if odd:
                kinds = ((far, 0), (planes, 2), (planes, 1))
            else:
                kinds = ((planes, 2), (planes, 1), (far, 1))
            rhs = jnp.concatenate([flat(ref, slot, n) for ref, n in kinds], axis=1)
            rows = pl.ds(pl.multiple_of(odd * chan_in + core * share, share), share)
            lhs = jnp.concatenate(
                [
                    turned[slot, a, rows, pl.ds(b * plane, cells)]
                    for a in range(3)
                    for b in range(3)
                ],
                axis=0,
            )
            piece = jnp.dot(lhs, rhs, preferred_element_type=jnp.float32)
            term = piece if term is None else term + piece
    for n in range(offsets // 3):
        for c in range(3):
            acc[pl.ds((3 * n + c) * units, units)] = term[
                n * share : (n + 1) * share, c * chan_out : (c + 1) * chan_out
            ].reshape(units, ROWS, chan_out)

    starts = [0]

    def span_of(stage, index):
        return pl.ds(starts[stage] + index * chunks[stage], chunks[stage])

    def offset_of(stage):
        return sum((stages[s][1] - 1) * chunks[s] for s in range(stage))

    def arrivals(stage):
        return pl.ds(offset_of(stage), (stages[stage][1] - 1) * chunks[stage])

    def at_last(target, name, last):
        if name == "chip":
            return (last * pair + core,) + target[1:]
        return target[:1] + ((last, target[2]) if name == "sx" else (target[1], last))

    def send_reduce(stage):
        group, count = stages[stage]
        chunk = chunks[stage]
        to, _, device = routes[stage]
        rows = pl.ds(starts[stage], count * chunk)
        leaving[rows] = encode(acc[rows])
        name = group[-1]
        deep_last = span(name, sizes)
        own_last = split(sizes, here)[name]
        for last in [k for k in reversed(range(deep_last)) if k % 2] + [k for k in range(deep_last) if k % 2 == 0]:
            step = (last - own_last + deep_last) % deep_last
            for first in reversed(range(0, count, deep_last)):
                index = to[first] - own_last + last
                copy = pltpu.make_async_remote_copy(
                    src_ref=leaving.at[span_of(stage, index)],
                    dst_ref=landing.at[pl.ds(offset_of(stage) + (first + step - 1) * chunk, chunk)],
                    send_sem=red_send.at[stage],
                    recv_sem=red_recv.at[stage],
                    device_id=at_last(device[first], name, last),
                    device_id_type=MESH,
                )
                if first:
                    copy.start()
                else:
                    pl.when(own_last != last)(copy.start)

    def take_reduce(stage):
        group, count = stages[stage]
        chunk = chunks[stage]
        own = starts[stage] + routes[stage][0][0] * chunk
        value = acc[pl.ds(own, chunk)]
        copies = whole(landing.at[arrivals(stage)], red_send.at[stage], red_recv.at[stage])
        copies.wait_recv()
        for turn in range(count - 1):
            value = value + decode(landing[pl.ds(offset_of(stage) + turn * chunk, chunk)])
        copies.wait_send()
        acc[pl.ds(own, chunk)] = value
        starts.append(own)

    def make_taps():
        loads[3].wait()
        blank = jnp.zeros((chan_in, chan_out), jnp.bfloat16)
        for n in range(offsets // 3):
            three = [weights_ref[3 * n + c] for c in range(3)]
            taps[n, pl.ds(0, chan_in)] = jnp.concatenate([blank] + three, axis=1)
            taps[n, pl.ds(chan_in, chan_in)] = jnp.concatenate(three + [blank], axis=1)

    def input_gradient():
        make_taps()
        halo_arrived(1)
        for odd in (0, 1):
            for row in (0, cells_y + 1):
                shift_z(0, odd, row, pl.ds(0, cells_x + 2))
            for col in (0, cells_x + 1):
                shift_z(0, odd, pl.ds(1, cells_y), col)
        sums = None
        for a in (-1, 0, 1):
            for b in (-1, 0, 1):
                ys, xs = pl.ds(1 - b, cells_y), pl.ds(1 - a, cells_x)
                lhs = jnp.concatenate(
                    [
                        ref[0, n, ys, xs].reshape(cells, LANES)
                        for ref, n in ((far, 0), (planes, 2), (planes, 1), (far, 1))
                    ],
                    axis=1,
                )
                piece = lax.dot_general(
                    lhs,
                    taps[3 * (a + 1) + b + 1],
                    (((1,), (1,)), ((), ())),
                    preferred_element_type=jnp.float32,
                )
                sums = piece if sums is None else sums + piece
        for row in range(cells_y):
            acts_wide[pl.ds(row, plane, stride=cells_y), :] = sums[row * plane : (row + 1) * plane]
        grad_ref[...] = acts_wide[...].astype(jnp.bfloat16).reshape(grad_ref.shape)

    for stage in range(depth):
        send_reduce(stage)
        if stage == 0:
            input_gradient()
        take_reduce(stage)

    own, chunk = starts[-1], chunks[-1]
    value = acc[pl.ds(own, chunk)] * (1.0 / (samples * sizes[0]))
    coded = encode(value)
    rest = pltpu.roll(value - decode(coded), 1, 1)
    unit = own + lax.broadcasted_iota(jnp.int32, value.shape, 0)
    row = lax.broadcasted_iota(jnp.int32, value.shape, 1)
    is_rest = jnp.logical_and(unit == bias_unit, row == 1)
    total[core, pl.ds(own, chunk)] = encode(jnp.where(is_rest, rest, value))

    def unfold(side, rows):
        wide_ref[side, rows] = decode(total[side, rows])

    def forward(part, rows):
        ref = total.at[core, rows]
        pltpu.make_async_remote_copy(
            src_ref=ref, dst_ref=ref, send_sem=fwd_send.at[0], recv_sem=fwd_recv.at[part],
            device_id=(mate, x, y), device_id_type=MESH,
        ).start()

    for stage in reversed(range(depth)):
        group, count = stages[stage]
        to, origin, device = routes[stage]
        me = to[0]
        ref = total.at[core, span_of(stage, me)]
        name = group[-1]
        deep_last = span(name, sizes)
        own_last = split(sizes, here)[name]
        firsts = list(reversed(range(0, count, deep_last)))
        nearby = {first: 0 for first in firsts}
        if len(group) > 1:
            nearby = {first: device[first][0] // pair + device[first][1] for first in firsts}
        for rank, first, last in itertools.product(range(NEAR + 1), firsts, range(deep_last)):
            if last > rank and rank < NEAR:
                continue
            copy = pltpu.make_async_remote_copy(
                src_ref=ref, dst_ref=ref, send_sem=gat_send.at[stage],
                recv_sem=gat_recv.at[stage * PARTS + first // deep_last],
                device_id=at_last(device[first], name, last), device_id_type=MESH,
            )
            steps = nearby[first] + last
            ok = (steps == rank) if rank < NEAR else (steps >= rank)
            if not first:
                ok = jnp.logical_and(ok, own_last != last)
            pl.when(ok)(copy.start)

        def sources(first):
            return [
                origin[first] - own_last + (own_last + turn) % deep_last
                for turn in range(0 if first else 1, deep_last)
            ]

        last = stage == 0
        if last and pair == 2:
            forward(0, span_of(stage, me))
        if stage == depth - 1:
            unfold(core, span_of(stage, me))
        for first in reversed(firsts):
            part = first // deep_last
            origins = sources(first)
            if not origins:
                continue
            ref = total.at[0, pl.ds(0, len(origins) * chunks[stage])]
            whole(ref, gat_send.at[stage], gat_recv.at[stage * PARTS + part]).wait_recv()
            if last and pair == 2:
                for index in origins:
                    forward(1 + part, span_of(stage, index))
            for index in origins:
                unfold(core, span_of(stage, index))
    if pair == 2:
        for part in range(len(firsts) + 1):
            origins = sources((part - 1) * deep_last) if part else [me]
            if not origins:
                continue
            ref = total.at[0, pl.ds(0, len(origins) * chunks[0])]
            whole(ref, fwd_send.at[0], fwd_recv.at[part]).wait_recv()
            for index in origins:
                unfold(1 - core, span_of(0, index))
    bias_ref[...] = wide_ref[0, bias_unit, pl.ds(0, 1)] + wide_ref[0, bias_unit, pl.ds(1, 1)]
    for stage in range(depth):
        ref = total.at[0, pl.ds(0, (stages[stage][1] - 1) * chunks[stage])]
        whole(ref, gat_send.at[stage], gat_recv.at[stage * PARTS]).wait_send()
    if pair == 2:
        whole(total.at[0], fwd_send.at[0], fwd_recv.at[0]).wait_send()
        ref = planes.at[0, :, *inner]
        whole(ref, pair_send.at[0], pair_recv.at[0]).wait_send()
    halo_left()


def fused(acts, before, upper, weights, cells_y, samples, sizes):
    cells_x, rows_acts, _ = acts.shape
    deep = rows_acts // cells_y
    offsets, chan_in, chan_out = weights.shape
    stages = plan_stages(sizes)
    pair = span("core", sizes)
    devices = 1
    for _, count in stages:
        devices *= count
    per_tap = chan_in // pair // ROWS
    step = math.lcm(devices, per_tap)
    units = -(-(offsets * per_tap + 1) // step) * step
    chunks = []
    for _, count in stages:
        chunks.append((chunks[-1] if chunks else units) // count)
    arriving = sum((count - 1) * chunk for (_, count), chunk in zip(stages, chunks))
    half, full = jnp.bfloat16, jnp.float32
    padded = (cells_y + 2, cells_x + 2, deep, LANES)
    cells = cells_x * rows_acts
    dma = pltpu.SemaphoreType.DMA
    lanes = (2 if sizes[1] <= 2 else 3) * (2 if sizes[2] <= 2 else 3) - 1
    scratch = [
        pltpu.VMEM(acts.shape, half),
        pltpu.VMEM(before.shape, half),
        pltpu.VMEM(upper.shape, half),
        pltpu.VMEM(weights.shape, half),
        pltpu.VMEM((cells, LANES), full),
        pltpu.VMEM((2 * cells, LANES), full),
        pltpu.VMEM((upper.shape[0] * upper.shape[1], LANES), full),
        pltpu.VMEM((pair, 3) + padded, half),
        pltpu.VMEM((pair, 2) + padded, half),
        pltpu.VMEM((2, pair, cells_x // 2, deep, LANES), half),
        pltpu.VMEM((2, pair, cells_x // 2, deep, LANES), half),
        pltpu.VMEM((2, pair, cells_y // 2, deep, LANES), half),
        pltpu.VMEM((2, pair, cells_y // 2, deep, LANES), half),
        pltpu.VMEM((pair, 3, LANES, (cells_y + 2) * cells_x * deep), half),
        pltpu.VMEM((offsets // 3, LANES, 4 * chan_out), half),
        pltpu.VMEM((units, ROWS, chan_out), full),
        pltpu.VMEM((pair, units, ROWS, chan_out), half),
        pltpu.VMEM((arriving, ROWS, chan_out), half),
        pltpu.VMEM((units, ROWS, chan_out), half),
        dma((4,)),
        dma((lanes,)),
        dma((2, lanes)),
        dma((1,)),
        dma((2,)),
        dma((len(stages),)),
        dma((len(stages),)),
        dma((len(stages),)),
        dma((len(stages) * PARTS,)),
        dma((1,)),
        dma((PARTS + 1,)),
    ]
    return pl.pallas_call(
        functools.partial(body, sizes, stages, chunks, samples),
        out_shape=(
            pltpu.VMEM(acts.shape, half),
            pltpu.VMEM((pair, units, ROWS, chan_out), full),
            pltpu.VMEM((1, chan_out), full),
        ),
        in_specs=[pl.BlockSpec(memory_space=pltpu.MemorySpace.HBM)] * 4,
        out_specs=(pl.BlockSpec(memory_space=pltpu.VMEM),) * 3,
        scratch_shapes=scratch,
        compiler_params=pltpu.CompilerParams(
            collective_id=0, has_side_effects=True, vmem_limit_bytes=VMEM_LIMIT
        ),
    )(acts, before, upper, weights)


def store(grad_in, wide_in, bias_in, grad_out, wide_out, bias_out, sems):
    pair, _, share, _ = wide_in.shape
    copies = [
        pltpu.make_async_copy(
            wide_in.at[side, pl.ds(0, wide_out.shape[0])],
            wide_out.at[:, pl.ds(side * share, share)],
            sems.at[2 + side],
        )
        for side in range(pair)
    ]
    copies.append(pltpu.make_async_copy(grad_in, grad_out, sems.at[0]))
    copies.append(pltpu.make_async_copy(bias_in, bias_out, sems.at[1]))
    for copy in copies:
        copy.start()
    for copy in copies:
        copy.wait()


def finish(grad, wide, bias, offsets):
    pair, _, share, chan_out = wide.shape
    return pl.pallas_call(
        store,
        out_shape=(
            jax.ShapeDtypeStruct(grad.shape, grad.dtype),
            jax.ShapeDtypeStruct((offsets, pair * share, chan_out), wide.dtype),
            jax.ShapeDtypeStruct(bias.shape, bias.dtype),
        ),
        in_specs=[pl.BlockSpec(memory_space=pltpu.VMEM)] * 3,
        out_specs=(pl.BlockSpec(memory_space=pltpu.MemorySpace.HBM),) * 3,
        scratch_shapes=[pltpu.SemaphoreType.DMA((2 + pair,))],
        compiler_params=pltpu.CompilerParams(vmem_limit_bytes=STORE_LIMIT),
    )(grad, wide, bias)


def fold(array):
    rows, cols, flat = array.shape
    array = array.reshape(rows, cols, flat // LANES, LANES).transpose(0, 2, 1, 3)
    return array.reshape(rows, flat // LANES * cols, LANES)


def on_device(sizes, activations, preact, pooled_grad, weights):
    samples, cells_x, cells_y, _ = activations.shape
    offsets, chan_in, chan_out = weights.shape
    acts = fold(activations.reshape(activations.shape[1:]))
    before = fold(preact.reshape(preact.shape[1:]))
    upper = fold(pooled_grad.reshape(pooled_grad.shape[1:]))
    grad, total, bias = fused(acts, before, upper, weights, cells_y, samples, sizes)
    pair = span("core", sizes)
    total = total.reshape(pair, -1, chan_in // pair, chan_out)
    grad, total, bias = finish(grad, total, bias, offsets)
    grad = grad.reshape(cells_x, -1, cells_y, LANES).transpose(0, 2, 1, 3)
    return (
        grad.reshape(activations.shape),
        total,
        bias.reshape(chan_out),
    )


def solution(mesh):
    sizes = tuple(mesh.shape[axis] for axis in AXES)
    placed = (P("dp", "sx", "sy", None), P("dp", "sx", "sy", None), P("dp", "sx", "sy", None), P())
    return jax.shard_map(
        functools.partial(on_device, sizes),
        mesh=mesh,
        in_specs=placed,
        out_specs=(P("dp", "sx", "sy", None), P(), P()),
        check_vma=False,
    )
```
